32 devices in a mesh: grp: 4 (over x, core), mem: 8 (over z, y).
Axes of the slice: x: 2, y: 2, z: 4, core: 2. Of those that a mesh axis runs over, the one named last changes fastest.
Arguments:
- embeddings: bfloat16 [16384, 768], P(('grp', 'mem')), may hold values from -1500 to 1500
- cluster_id: int32 [16384], P(('grp', 'mem')), may hold values from 0 to 3, as said below
- row_order: int32 [16384], P(('grp', 'mem')), may hold values from 0 to 16383, each once
- assignment: int32 [4], replicated, may hold values from 0 to 3, as said below
- placement: int32 [16384], P(('grp', 'mem')), may hold values from 0 to 7
Outputs:
- owner_best: float32 [32768], P(('grp', 'mem'))
The draws below stay inside these ranges and needn't reach their ends.
Inputs may be any that keep to these rules, and one draw needn't show every extreme that they name: `cluster_id`: owner = assignment * 8 + placement; at most 32 rows of one device share an owner, and in every draw some owner gets exactly 32 rows from every device. `assignment`: each group owns exactly 1 cluster.
All inputs are finite; a program needn't handle non-finite values.
Results may differ from the reference program's by a relative error of at most 0.00034.
Values may be sent and summed in bfloat16 or wider, within the bound.
A program may use at most 128 MiB of HBM per device.

```python
import math
import jax
import jax.numpy as jnp
from jax import lax

D = 768
ROWS_DEV = 512
CL_GRP = 1
GROUPS = 4
MEMBERS = 8
OWNERS = 32
CAP = 32
SLOTS = 1024
ROWS = 16384
CLUSTERS = 4


def route_plan(key):
    base_key = jax.random.fold_in(key, 5)
    key_perm, key_hot, key_dest, key_pick = jax.random.split(base_key, 4)
    shuffled = jax.random.permutation(key_perm, CLUSTERS)
    assignment = shuffled % GROUPS
    listing = jnp.argsort(shuffled)
    hot_owner = jax.random.randint(key_hot, (), 0, OWNERS)
    others = jnp.arange((OWNERS - 1) * CAP) // CAP
    others = others + (others >= hot_owner).astype(others.dtype)

    def per_source(source_key):
        key_take, key_mix = jax.random.split(source_key)
        picked = jax.random.permutation(key_take, (OWNERS - 1) * CAP)[:ROWS_DEV - CAP]
        targets = jnp.concatenate([jnp.full((CAP,), hot_owner, others.dtype), others[picked]])
        return jax.random.permutation(key_mix, targets)
    targets = jax.vmap(per_source)(jax.random.split(key_dest, OWNERS)).reshape(ROWS)
    within = jax.random.randint(key_pick, (ROWS,), 0, CL_GRP)
    cluster_id = listing[targets // MEMBERS + GROUPS * within]
    placement = targets % MEMBERS
    return (cluster_id.astype(jnp.int32), assignment.astype(jnp.int32), placement.astype(jnp.int32))


def draw_cluster_id(key, part):
    return route_plan(key)[0]


def draw_assignment(key, part):
    return route_plan(key)[1]


def draw_placement(key, part):
    return route_plan(key)[2]


def draw_embeddings(key, part):
    cluster_id = route_plan(key)[0]
    key_base, key_shared, key_weight, key_scale = jax.random.split(jax.random.fold_in(key, 11), 4)
    noise = jax.random.truncated_normal(key_base, -4.0, 4.0, (ROWS, D), jnp.float32)
    shared = jax.random.truncated_normal(key_shared, -4.0, 4.0, (ROWS, D), jnp.float32)
    sorter = jnp.argsort(cluster_id, stable=True)
    sorted_ids = cluster_id[sorter]
    position = jnp.arange(ROWS)
    partner = jnp.minimum(position ^ 1, ROWS - 1)
    paired = sorted_ids[partner] == sorted_ids
    anchor_sorted = jnp.where(paired, sorter[jnp.minimum(position, partner)], sorter)
    anchor = jnp.zeros((ROWS,), jnp.int32).at[sorter].set(anchor_sorted.astype(jnp.int32))
    weight = jax.random.uniform(key_weight, (ROWS, 1), jnp.float32, 1.0, 4.0)
    values = noise + weight * shared[anchor]
    row_scale = jnp.exp(jax.random.uniform(key_scale, (ROWS, 1), jnp.float32, 0.0, 2.302585))
    return (values * row_scale).astype(jnp.bfloat16)


def setup_inputs(seed: int = 0) -> dict:
    seeds = jax.random.split(jax.random.key(seed), 6)
    embeddings = draw_embeddings(jax.random.fold_in(seeds[5], 71), 0)
    cluster_id = draw_cluster_id(jax.random.fold_in(seeds[5], 71), 0)
    row_order = jax.random.permutation(seeds[2], ROWS).astype(jnp.int32)
    assignment = draw_assignment(jax.random.fold_in(seeds[5], 71), 0)
    placement = draw_placement(jax.random.fold_in(seeds[5], 71), 0)
    return dict(embeddings=embeddings, cluster_id=cluster_id, row_order=row_order, assignment=assignment, placement=placement)


def reference(embeddings, cluster_id, row_order, assignment, placement):
    widened = embeddings.astype(jnp.float32)
    feature_count = widened.shape[1]
    rounded = (widened * lax.rsqrt(lax.optimization_barrier(jnp.mean(widened * widened, axis=1, keepdims=True)) + 1e-06) * (1.0 / math.sqrt(feature_count))).astype(jnp.bfloat16)
    unit_rows = lax.optimization_barrier(rounded).astype(jnp.float32)
    row_count = unit_rows.shape[0]
    block_rows = 512 if row_count % 512 == 0 else row_count
    blocks = row_count // block_rows

    def block_max(packed):
        block_units, block_cluster, block_order = packed
        scores = jnp.dot(block_units, unit_rows.T, precision=lax.Precision.HIGHEST)
        eligible = (block_cluster[:, None] == cluster_id[None, :]) & (row_order[None, :] < block_order[:, None])
        return jnp.maximum(lax.optimization_barrier(jnp.max(jnp.where(eligible, scores, -2.0), axis=1)), -1.0)
    similar = lax.map(block_max, (unit_rows.reshape(blocks, block_rows, feature_count), cluster_id.reshape(blocks, block_rows), row_order.reshape(blocks, block_rows))).reshape(row_count)
    owner_id = (assignment[cluster_id] * MEMBERS + placement).astype(jnp.int32).reshape(OWNERS, ROWS_DEV)
    owner_hits = (owner_id[:, :, None] == jnp.arange(OWNERS).astype(jnp.int32)[None, None, :]).astype(jnp.int32)
    rank_in_source = lax.optimization_barrier(jnp.sum((jnp.cumsum(owner_hits, axis=1) - 1) * owner_hits, axis=2)).astype(jnp.int32)
    source_id = jnp.arange(OWNERS).astype(jnp.int32)[:, None]
    slot_index = (owner_id * SLOTS + source_id * CAP + rank_in_source).reshape(row_count).astype(jnp.int32)
    return jnp.full((OWNERS * SLOTS,), -1.0, jnp.float32).at[slot_index].set(similar)
```

```python
import functools
import math

import jax
import jax.numpy as jnp
from jax import lax
from jax.experimental import pallas as pl
from jax.experimental.pallas import tpu as pltpu
from jax.sharding import PartitionSpec as P

MESH = pl.DeviceIdType.MESH
NZ = 4
CHUNKS = 4
TILE = 256
LOW = -2.0


def flip(index, mask):
    out, bit = index, 1
    while bit <= mask:
        if mask & bit:
            out = out + bit - 2 * bit * (lax.div(index, bit) % 2)
        bit *= 2
    return out


def kernel(
    groups, ys, units, meta, best, planes, zs, plane_meta, z_meta, col_acc, row_acc,
    row_key, row_cluster, back, z_back, z_send, ready_sem, p_send, p_recv, z_ssem, z_rsem,
    pm_send, pm_recv, zm_send, zm_recv, b_send, b_recv, zb_send, zb_recv, relay_sem,
):
    g, m = lax.axis_index("grp"), lax.axis_index("mem")
    z, y = lax.div(m, ys), m % ys
    tiles = (groups // 2) * ys
    count = 2 * tiles
    rows = planes.shape[1]
    part = rows // CHUNKS

    def plane_peer(d):
        j, c = d // 2, d % 2
        return (flip(g, (j // ys) * 2 + c), z * ys + flip(y, j % ys))

    def column_peer(dz):
        return (g, ((z + dz) % NZ) * ys + y)

    load = pltpu.make_async_copy(units, planes.at[0], ready_sem)
    load.start()

    barrier = pltpu.get_barrier_semaphore()
    peers = [plane_peer(d) for d in range(1, count)] + [column_peer(k) for k in range(1, NZ)]
    for peer in peers:
        pl.semaphore_signal(barrier, inc=1, device_id=peer, device_id_type=MESH)
    col_acc[...] = jnp.full(col_acc.shape, LOW, jnp.float32)
    row_acc[...] = jnp.full(row_acc.shape, LOW, jnp.float32)
    plane_meta[0] = meta[...]
    load.wait()
    pl.semaphore_wait(barrier, len(peers))

    def remote(src, dst, ssem, rsem, peer):
        return pltpu.make_async_remote_copy(
            src_ref=src, dst_ref=dst, send_sem=ssem, recv_sem=rsem,
            device_id=peer, device_id_type=MESH,
        )

    def piece(k):
        return pl.ds(k * part, part)

    def own_to_z(k, slot, dz):
        return remote(
            planes.at[0, piece(k)], zs.at[slot, piece(k)], z_ssem.at[slot, k],
            z_rsem.at[slot, k], column_peer(dz),
        )

    def relay(k, src, dst, dz):
        return remote(
            zs.at[src, piece(k)], zs.at[dst, piece(k)], relay_sem.at[src, k],
            z_rsem.at[dst, k], column_peer(dz),
        )

    def to_plane(d):
        return remote(planes.at[0], planes.at[d], p_send.at[d], p_recv.at[d], plane_peer(d))

    def forward(j):
        return remote(
            planes.at[2 * j], planes.at[2 * j + 1], p_send.at[2 * j + 1], p_recv.at[2 * j + 1],
            plane_peer(1),
        )

    meta_copies = [
        remote(meta, plane_meta.at[d], pm_send.at[d], pm_recv.at[d], plane_peer(d))
        for d in range(1, count)
    ] + [
        remote(meta, z_meta.at[s], zm_send.at[s], zm_recv.at[s], column_peer(-1 - s))
        for s in range(2)
    ]
    for copy in meta_copies:
        copy.start()

    to_plane(1).start()

    @pl.when(z >= 1)
    def _():
        for k in range(CHUNKS):
            own_to_z(k, 0, -1).start()

    @pl.when(z <= 1)
    def _():
        for k in range(CHUNKS):
            own_to_z(k, 1, 2).start()

    for j in range(1, tiles):
        to_plane(2 * j).start()

    def spread(a, source):
        row_key[a] = jnp.broadcast_to(source[0:1, :], (128, rows)).T
        row_cluster[a] = jnp.broadcast_to(source[1:2, :], (128, rows)).T

    def pairs(a, left, d, both):
        right = planes[d]
        keys, clusters = plane_meta[d, 0:1, :], plane_meta[d, 1:2, :]

        def step(i, carry):
            here = pl.ds(pl.multiple_of(i * TILE, TILE), TILE)
            scores = lax.dot_general(
                left[here, :], right, (((1,), (1,)), ((), ())),
                preferred_element_type=jnp.float32,
            )
            my_key, my_cluster = row_key[a, here, :], row_cluster[a, here, :]
            acc = row_acc[a, here, :]
            for t in range(rows // 128):
                lanes = slice(t * 128, (t + 1) * 128)
                kept = jnp.where(my_cluster == clusters[:, lanes], scores[:, lanes], LOW)
                earlier = keys[:, lanes] < my_key
                acc = jnp.maximum(acc, jnp.where(earlier, kept, LOW))
                if both:
                    other = jnp.where(earlier, LOW, kept).reshape(TILE // 8, 8, 128)
                    col_acc[d, :, lanes] = jnp.maximum(col_acc[d, :, lanes], jnp.max(other, axis=0))
            row_acc[a, here, :] = acc
            return carry

        lax.fori_loop(0, rows // TILE, step, 0)

    spread(0, meta)
    own = planes.at[0]
    pairs(0, own, 0, False)
    for copy in meta_copies:
        copy.wait()
    to_plane(1).wait_recv()
    pairs(0, own, 1, False)

    for k in range(CHUNKS):
        @pl.when((z == 1) | (z == 2))
        def _():
            own_to_z(k, 0, -1).wait_recv()
            relay(k, 0, 1, -1).start()

        @pl.when(z == 2)
        def _():
            own_to_z(k, 1, 2).wait_recv()
            relay(k, 1, 0, 1).start()

    def plane_step(j, carry):
        pltpu.make_async_copy(planes.at[2 * j], planes.at[2 * j], p_recv.at[2 * j]).wait()
        forward(j).start()
        pairs(0, own, 2 * j, False)
        forward(j).wait_recv()
        pairs(0, own, 2 * j + 1, False)
        return carry

    lax.fori_loop(1, tiles, plane_step, 0)

    for k in range(CHUNKS):
        @pl.when((z == 0) | (z == 3))
        def _():
            own_to_z(k, 0, -1).wait_recv()

        @pl.when(z != 2)
        def _():
            own_to_z(k, 1, 2).wait_recv()

    spread(1, z_meta.at[0])
    spread(2, z_meta.at[1])

    def z1_step(d, carry):
        pairs(1, zs.at[0], d, True)
        return carry

    lax.fori_loop(0, count, z1_step, 0)
    first = lax.div(z, 2) * (count // 2)

    def z2_step(d, carry):
        pairs(2, zs.at[1], d + first, True)
        return carry

    lax.fori_loop(0, count // 2, z2_step, 0)

    def fold(a):
        return jnp.max(row_acc[a].T.reshape(16, 8, rows), axis=0)

    z_send[0] = fold(1)
    z_send[1] = fold(2)
    result_copies = [
        remote(col_acc.at[d], back.at[d], b_send.at[d], b_recv.at[d], plane_peer(d))
        for d in range(1, count)
    ]
    for copy in result_copies:
        copy.start()
    mine = jnp.maximum(fold(0), col_acc[0])
    z_copies = [
        remote(z_send.at[s], z_back.at[s], zb_send.at[s], zb_recv.at[s], column_peer(1 + s))
        for s in range(2)
    ]
    for copy in z_copies:
        copy.start()

    @pl.when(z >= 1)
    def _():
        for k in range(CHUNKS):
            own_to_z(k, 0, -1).wait_send()

    @pl.when(z <= 1)
    def _():
        for k in range(CHUNKS):
            own_to_z(k, 1, 2).wait_send()

    @pl.when((z == 1) | (z == 2))
    def _():
        for k in range(CHUNKS):
            relay(k, 0, 1, -1).wait_send()

    @pl.when(z == 2)
    def _():
        for k in range(CHUNKS):
            relay(k, 1, 0, 1).wait_send()

    to_plane(1).wait_send()
    for j in range(1, tiles):
        to_plane(2 * j).wait_send()
        forward(j).wait_send()

    for copy in result_copies + z_copies:
        copy.wait()
    for d in range(1, count):
        mine = jnp.maximum(mine, back[d])
    mine = jnp.maximum(mine, jnp.maximum(z_back[0], z_back[1]))
    best[...] = jnp.maximum(jnp.max(mine, axis=0, keepdims=True), -1.0)


def similarities(units, meta, groups, members):
    rows, width = units.shape
    ys = members // NZ
    count = groups * ys
    dma = pltpu.SemaphoreType.DMA
    return pl.pallas_call(
        functools.partial(kernel, groups, ys),
        out_shape=jax.ShapeDtypeStruct((1, rows), jnp.float32),
        in_specs=[
            pl.BlockSpec(memory_space=pl.ANY),
            pl.BlockSpec(memory_space=pltpu.VMEM),
        ],
        out_specs=pl.BlockSpec(memory_space=pltpu.VMEM),
        scratch_shapes=[
            pltpu.VMEM((count, rows, width), jnp.bfloat16),
            pltpu.VMEM((2, rows, width), jnp.bfloat16),
            pltpu.VMEM((count, 2, rows), jnp.float32),
            pltpu.VMEM((2, 2, rows), jnp.float32),
            pltpu.VMEM((count, 8, rows), jnp.float32),
            pltpu.VMEM((3, rows, 128), jnp.float32),
            pltpu.VMEM((3, rows, 128), jnp.float32),
            pltpu.VMEM((3, rows, 128), jnp.float32),
            pltpu.VMEM((count, 8, rows), jnp.float32),
            pltpu.VMEM((2, 8, rows), jnp.float32),
            pltpu.VMEM((2, 8, rows), jnp.float32),
            dma(()),
            dma((count,)), dma((count,)),
            dma((2, CHUNKS)), dma((2, CHUNKS)),
            dma((count,)), dma((count,)),
            dma((2,)), dma((2,)),
            dma((count,)), dma((count,)),
            dma((2,)), dma((2,)),
            dma((2, CHUNKS)),
        ],
        compiler_params=pltpu.CompilerParams(
            collective_id=1, has_side_effects=True, vmem_limit_bytes=56 * 1024 * 1024
        ),
    )(units, meta)


HELD = 176
LAYOUT = 768
BIG = 1e9
STEPS = ((0, 384), (384, 128), (512, 128), (640, 128))
FILLED = ((0, 352), (384, 128), (512, 128), (640, 96))
FAR = {2: ((384, 64), (512, 64), (640, 48)), 3: ((448, 64), (576, 64), (688, 48))}
NEAR = (176, 176)


def relation_of(place):
    far = (place >= 448) & (place < 512) | (place >= 576) & (place < 640) | (place >= 688)
    return jnp.where(place < 176, 0, jnp.where(place < 352, 1, jnp.where(far, 3, 2)))


def either(a, b):
    return a + b - 2 * a * b


def routed_kernel(
    assignment, embeddings, cluster, order, member, out, over,
    raw, units, sent, blocks, sent_meta, z_meta, metas, row_key, row_acc, col_acc,
    places, fin, fin_got, load_sem, zs, zr, mzs, mzr, ps, pr, mps, mpr, fs, fr,
):
    g, m = lax.axis_index("grp"), lax.axis_index("mem")
    x, c, z, y = lax.div(g, 2), g % 2, lax.div(m, 2), m % 2
    rows, width = raw.shape
    owners, capacity = 32, 32

    load = pltpu.make_async_copy(embeddings, raw, load_sem)
    load.start()

    def device(x, c, z, y):
        return (x * 2 + c, z * 2 + y)

    def column(j):
        return device(x, c, flip(z, j), y)

    side_to = (
        device(x, 1 - c, z, y),
        device(1 - x, either(c, 1 - x), z, y),
        device(x, either(either(c, x), 1 - y), z, 1 - y),
    )
    side_from = (
        device(x, 1 - c, z, y),
        device(1 - x, either(c, x), z, y),
        device(x, either(either(c, x), y), z, 1 - y),
    )
    here = x * 4 + y * 2 + c

    def home(i):
        return device(i // 4, i % 2, g, (i // 2) % 2)

    is_home = z == g
    barrier = pltpu.get_barrier_semaphore()
    for peer in [column(j) for j in (1, 2, 3)] + list(side_from):
        pl.semaphore_signal(barrier, inc=1, device_id=peer, device_id_type=MESH)
    for i in range(8):
        @pl.when(jnp.logical_not(is_home & (here == i)))
        def _():
            pl.semaphore_signal(barrier, inc=1, device_id=home(i), device_id_type=MESH)

    def remote(src, dst, ssem, rsem, peer):
        return pltpu.make_async_remote_copy(
            src_ref=src, dst_ref=dst, send_sem=ssem, recv_sem=rsem,
            device_id=peer, device_id_type=MESH,
        )

    def z_copy(j, k):
        start, size = NEAR if j == 1 else FAR[j][k]
        here = pl.ds(start, size)
        return remote(sent.at[here], blocks.at[0, here], zs.at[j, k], zr.at[j, k], column(j))

    def z_meta_copy(j):
        return remote(sent_meta, z_meta.at[j], mzs.at[j], mzr.at[j], column(j))

    PIECES = ((0, 176), NEAR) + FILLED[1:]

    def side_copy(t, k):
        here = pl.ds(*PIECES[k])
        return remote(
            blocks.at[0, here], blocks.at[t + 1, here], ps.at[t, k], pr.at[t, k], side_to[t]
        )

    def side_meta_copy(t):
        return remote(metas.at[0], metas.at[t + 1], mps.at[t], mpr.at[t], side_to[t])

    def fin_copy(p):
        return remote(fin.at[p], fin_got.at[here], fs.at[p], fr.at[here], (z, p))

    def fin_from(i):
        return remote(fin.at[0], fin_got.at[i], fs.at[0], fr.at[i], home(i))

    def wide(ref):
        return jnp.concatenate([ref[i : i + 1, :] for i in range(rows // 128)], axis=1)

    ids, keys, mem_of = wide(cluster), wide(order), wide(member)
    group = jnp.zeros_like(ids)
    for k in range(4):
        group = jnp.where(ids == k, assignment[k], group)
    owner = group * 8 + mem_of
    hits = jnp.concatenate(
        [
            (lax.broadcasted_iota(jnp.int32, (owners, rows), 0) == owner).astype(jnp.float32),
            (lax.broadcasted_iota(jnp.int32, (16, rows), 0) == group).astype(jnp.float32),
        ],
        axis=0,
    )
    before = (
        lax.broadcasted_iota(jnp.int32, (rows, rows), 0)
        < lax.broadcasted_iota(jnp.int32, (rows, rows), 1)
    ).astype(jnp.float32).astype(jnp.bfloat16)
    counts = hits * jnp.dot(
        hits.astype(jnp.bfloat16), before, preferred_element_type=jnp.float32
    )
    rank = jnp.sum(counts[:owners], axis=0, keepdims=True)
    pos = jnp.sum(counts[owners:], axis=0, keepdims=True).astype(jnp.int32)
    j = jnp.bitwise_xor(group, z)
    high = jnp.where(j >= 3, 1, 0)
    far = jnp.where(
        pos < 64, 384 + 64 * high + pos,
        jnp.where(pos < 128, 448 + 64 * high + pos, 512 + 48 * high + pos),
    )
    target = jnp.where(j == 0, pos, jnp.where(j == 1, 176 + pos, far))
    target = jnp.where(pos < HELD, target, -1)
    spilled = jnp.max(jnp.where(pos < HELD, 0.0, 1.0), axis=1, keepdims=True)

    def chosen(start, size):
        place = lax.broadcasted_iota(jnp.int32, (size, rows), 0) + start
        return (place == target).astype(jnp.float32).astype(jnp.bfloat16)

    facts = jnp.concatenate(
        [
            lax.shift_right_logical(keys, 8).astype(jnp.float32),
            jnp.bitwise_and(keys, 255).astype(jnp.float32),
            mem_of.astype(jnp.float32),
            rank,
            jnp.ones((1, rows), jnp.float32),
            jnp.zeros((11, rows), jnp.float32),
        ],
        axis=0,
    ).astype(jnp.bfloat16)
    for start, size in STEPS:
        lanes = slice(start, start + size)
        sorted_facts = lax.dot_general(
            facts, chosen(start, size), (((1,), (1,)), ((), ())),
            preferred_element_type=jnp.float32,
        )
        held = sorted_facts[4:5] > 0.5
        sent_meta[0:1, lanes] = jnp.where(
            held, sorted_facts[0:1] * 256.0 + sorted_facts[1:2], BIG
        )
        sent_meta[1:2, lanes] = jnp.where(held, sorted_facts[2:3], -1.0)
        sent_meta[2:3, lanes] = sorted_facts[3:4]
        sent_meta[3:4, lanes] = jnp.broadcast_to(spilled, (1, size))
        sent_meta[4:8, lanes] = jnp.zeros((4, size), jnp.float32)

    load.wait()

    def normalise(i, carry):
        part = pl.ds(pl.multiple_of(i * 128, 128), 128)
        widened = raw[part, :].astype(jnp.float32)
        scale = lax.rsqrt(jnp.mean(widened * widened, axis=1, keepdims=True) + 1e-06)
        units[part, :] = (widened * scale * (1.0 / math.sqrt(width))).astype(jnp.bfloat16)
        return carry

    lax.fori_loop(0, rows // 128, normalise, 0)

    def place(start, size):
        return jnp.dot(
            chosen(start, size), units[...], preferred_element_type=jnp.float32
        ).astype(jnp.bfloat16)

    @pl.when(is_home)
    def _():
        pl.semaphore_wait(barrier, 13)

    @pl.when(jnp.logical_not(is_home))
    def _():
        pl.semaphore_wait(barrier, 14)

    for k in range(2):
        start, size = STEPS[k + 1]
        sent[pl.ds(start, size), :] = place(start, size)
        z_copy(3, k).start()
        z_copy(2, k).start()
        if k == 0:
            for r in (1, 2, 3):
                z_meta_copy(r).start()
    near = place(0, 384)
    sent[pl.ds(*NEAR), :] = near[176:352]
    z_copy(1, 0).start()
    blocks[0, pl.ds(0, 176), :] = near[:176]
    for t in range(3):
        side_copy(t, 0).start()
    sent[pl.ds(640, 128), :] = place(640, 128)
    for b in range(4):
        for start, size in ((352, 32), (736, 32)):
            blocks[b, pl.ds(start, size), :] = jnp.zeros((size, width), jnp.bfloat16)
    row_acc[...] = jnp.full(row_acc.shape, LOW, jnp.float32)
    col_acc[...] = jnp.full(col_acc.shape, LOW, jnp.float32)

    for r in (1, 2, 3):
        z_meta_copy(r).wait_recv()
    lane = lax.broadcasted_iota(jnp.int32, (8, LAYOUT), 1)
    relation = relation_of(lane)
    joined = sent_meta[...]
    spill = jnp.max(joined[3:4], axis=1, keepdims=True)
    for r in (1, 2, 3):
        joined = jnp.where(relation == r, z_meta[r], joined)
        spill = jnp.maximum(spill, jnp.max(z_meta[r, 3:4, :], axis=1, keepdims=True))
    metas[0] = joined
    for t in range(3):
        side_meta_copy(t).start()

    def prepare(b):
        row_key[b] = jnp.broadcast_to(metas[b, 0:1, :], (128, LAYOUT)).T
        rel = relation[0:1]
        from_z = jnp.bitwise_xor(rel, z)
        slot = from_z * 32 + metas[b, 2:3, :].astype(jnp.int32)
        places[b] = (
            lax.broadcasted_iota(jnp.int32, (128, LAYOUT), 0) == slot
        ).astype(jnp.float32).astype(jnp.bfloat16)

    def pairs(left, left_rows, right, right_start, right_rows, both):
        span = slice(right_start, right_start + right_rows)
        their_key = metas[right, 0:1, span]
        theirs = blocks[right, pl.ds(right_start, right_rows), :]
        first, count = left_rows

        def step(i, carry):
            part = pl.ds(pl.multiple_of(first + i * 128, 128), 128)
            scores = lax.dot_general(
                blocks[left, part, :], theirs, (((1,), (1,)), ((), ())),
                preferred_element_type=jnp.float32,
            )
            my_key = row_key[left, part, :]
            acc = row_acc[left, part, :]
            for t in range(right_rows // 128):
                lanes = slice(t * 128, (t + 1) * 128)
                col = slice(right_start + t * 128, right_start + (t + 1) * 128)
                earlier = their_key[:, lanes] < my_key
                acc = jnp.maximum(acc, jnp.where(earlier, scores[:, lanes], LOW))
                if both:
                    other = jnp.where(earlier, LOW, scores[:, lanes]).reshape(16, 8, 128)
                    col_acc[right, :, col] = jnp.maximum(
                        col_acc[right, :, col], jnp.max(other, axis=0)
                    )
            row_acc[left, part, :] = acc
            return carry

        lax.fori_loop(0, count // 128, step, 0)

    def own_step(s):
        start, size = STEPS[s]
        if s:
            pairs(0, (0, start), 0, start, size, True)
        pairs(0, (start, size), 0, start, size, False)

    def side_step(s):
        start, size = STEPS[s]
        pairs(0, (0, start + size), 1, start, size, True)
        for left, right in ((0, 2), (0, 3), (2, 3)):
            pairs(left, (0, start + size), right, start, size, True)
            if s:
                pairs(right, (0, start), left, start, size, True)

    z_copy(1, 0).wait_recv()
    for t in range(3):
        side_copy(t, 1).start()
    prepare(0)
    own_step(0)
    for s in (1, 2, 3):
        for r in (3, 2):
            z_copy(r, s - 1).wait_recv()
        for t in range(3):
            side_copy(t, s + 1).start()
        if s == 1:
            for r in (3, 2):
                z_copy(r, 0).wait_send()
                z_copy(r, 2).start()
            for t in range(3):
                side_meta_copy(t).wait_recv()
            for b in (1, 2, 3):
                prepare(b)
            for t in range(3):
                side_copy(t, 0).wait_recv()
        for t in range(3):
            side_copy(t, s).wait_recv()
        side_step(s - 1)
        own_step(s)
    for t in range(3):
        side_copy(t, 4).wait_recv()
    side_step(3)

    for b in range(4):
        value = jnp.max(col_acc[b], axis=0, keepdims=True)
        if b != 1:
            value = jnp.maximum(value, jnp.max(row_acc[b].T, axis=0, keepdims=True))
        value = jnp.maximum(value, -1.0)
        parts = []
        for _ in range(3):
            part = value.astype(jnp.bfloat16).astype(jnp.float32)
            parts.append(part)
            value = value - part
        parts.append(jnp.ones_like(value))
        mine = (
            lax.broadcasted_iota(jnp.int32, (8, LAYOUT), 0)
            == metas[b, 1:2, :].astype(jnp.int32)
        ).astype(jnp.float32)
        stacked = jnp.concatenate([mine * part for part in parts], axis=0).astype(jnp.bfloat16)
        found = lax.dot_general(
            stacked, places[b], (((1,), (1,)), ((), ())), preferred_element_type=jnp.float32
        )
        total = (found[16:24] + found[8:16]) + found[0:8]
        fin[:, b, :] = jnp.where(found[24:32] > 0.5, total, -1.0)
    for b in range(4, 8):
        fin[:, b, :] = jnp.broadcast_to(spill, (8, 128))

    for p in range(8):
        me = is_home & (m == p)

        @pl.when(jnp.logical_not(me))
        def _():
            fin_copy(p).start()

        @pl.when(me)
        def _():
            fin_got[here] = fin[p]

    for r in (1, 2, 3):
        z_meta_copy(r).wait_send()
    z_copy(1, 0).wait_send()
    for r in (3, 2):
        for k in (1, 2):
            z_copy(r, k).wait_send()
    for t in range(3):
        side_meta_copy(t).wait_send()
        for k in range(5):
            side_copy(t, k).wait_send()
    for p in range(8):
        @pl.when(jnp.logical_not(is_home & (m == p)))
        def _():
            fin_copy(p).wait_send()
    for i in range(8):
        @pl.when(jnp.logical_not(is_home & (here == i)))
        def _():
            fin_from(i).wait_recv()

    block = lax.broadcasted_iota(jnp.int32, (1, 128), 1) // 32
    worst = fin_got[0, 4:5, :]
    for i in range(1, 8):
        worst = jnp.maximum(worst, fin_got[i, 4:5, :])
    over[...] = jnp.broadcast_to(worst, (8, 128))
    for xs in range(2):
        for cs in range(2):
            ways = []
            for ys in range(2):
                i = xs * 4 + ys * 2 + cs
                sibling = xs * 4 + ys * 2 + (1 - cs)
                x_holder = (1 - xs) * 4 + ys * 2 + (cs ^ (1 - xs))
                y_holder = xs * 4 + (1 - ys) * 2 + (cs ^ xs ^ (1 - ys))
                ways.append(
                    jnp.maximum(
                        jnp.maximum(fin_got[i, 0:1, :], fin_got[sibling, 1:2, :]),
                        jnp.maximum(fin_got[x_holder, 2:3, :], fin_got[y_holder, 3:4, :]),
                    )
                )
            for half, turns in enumerate(((0, 32, 32, 64), (64, 96, 96, 0))):
                line = ways[0]
                for k in range(4):
                    way = ways[k % 2]
                    turned = pltpu.roll(way, turns[k], 1) if turns[k] else way
                    line = jnp.where(block == k, turned, line)
                row = (xs * 2 + cs) * 2 + half
                out[row : row + 1, :] = line


def routed(embeddings, cluster_id, row_order, assignment, placement):
    rows, width = embeddings.shape
    dma = pltpu.SemaphoreType.DMA
    lines = (rows // 128, 128)
    vmem = pl.BlockSpec(memory_space=pltpu.VMEM)
    return pl.pallas_call(
        routed_kernel,
        out_shape=[jax.ShapeDtypeStruct((8, 128), jnp.float32)] * 2,
        in_specs=[
            pl.BlockSpec(memory_space=pltpu.SMEM), pl.BlockSpec(memory_space=pl.ANY),
            vmem, vmem, vmem,
        ],
        out_specs=[vmem, vmem],
        scratch_shapes=[
            pltpu.VMEM((rows, width), jnp.bfloat16),
            pltpu.VMEM((rows, width), jnp.bfloat16),
            pltpu.VMEM((LAYOUT, width), jnp.bfloat16),
            pltpu.VMEM((4, LAYOUT, width), jnp.bfloat16),
            pltpu.VMEM((8, LAYOUT), jnp.float32),
            pltpu.VMEM((4, 8, LAYOUT), jnp.float32),
            pltpu.VMEM((4, 8, LAYOUT), jnp.float32),
            pltpu.VMEM((4, LAYOUT, 128), jnp.float32),
            pltpu.VMEM((4, LAYOUT, 128), jnp.float32),
            pltpu.VMEM((4, 8, LAYOUT), jnp.float32),
            pltpu.VMEM((4, 128, LAYOUT), jnp.bfloat16),
            pltpu.VMEM((8, 8, 128), jnp.float32),
            pltpu.VMEM((8, 8, 128), jnp.float32),
            dma(()),
            dma((4, 3)), dma((4, 3)),
            dma((4,)), dma((4,)),
            dma((3, 5)), dma((3, 5)),
            dma((3,)), dma((3,)),
            dma((8,)), dma((8,)),
        ],
        compiler_params=pltpu.CompilerParams(
            collective_id=0, has_side_effects=True, vmem_limit_bytes=48 * 1024 * 1024
        ),
    )(
        assignment, embeddings, cluster_id.reshape(lines), row_order.reshape(lines),
        placement.reshape(lines),
    )


def dense(embeddings, cluster_id, row_order, assignment, placement):
    members = lax.axis_size("mem")
    groups = lax.axis_size("grp")
    owners = groups * members
    row_count, feature_count = embeddings.shape
    capacity = max(2, 2 * row_count // owners)
    widened = embeddings.astype(jnp.float32)
    unit_rows = (
        widened
        * lax.rsqrt(jnp.mean(widened * widened, axis=1, keepdims=True) + 1e-06)
        * (1.0 / math.sqrt(feature_count))
    ).astype(jnp.bfloat16)
    meta = jnp.stack([row_order, cluster_id]).astype(jnp.float32)
    best = similarities(unit_rows, meta, groups, members)

    table_hits = cluster_id[:, None] == jnp.arange(assignment.shape[0], dtype=jnp.int32)[None, :]
    group_of = jnp.sum(jnp.where(table_hits, assignment[None, :], 0), axis=1)
    owner_id = group_of * members + placement
    before = jnp.arange(row_count)[None, :] < jnp.arange(row_count)[:, None]
    rank = jnp.sum((before & (owner_id[None, :] == owner_id[:, None])).astype(jnp.int32), axis=1)
    target = owner_id * capacity + rank
    slots = jnp.arange(owners * capacity, dtype=jnp.int32)
    filled = jnp.max(
        jnp.where(slots[:, None] == target[None, :], best, -1.0), axis=1
    )
    return lax.all_to_all(filled, ("grp", "mem"), split_axis=0, concat_axis=0, tiled=True)


def local(*args):
    embeddings, _, _, assignment, _ = args
    shape = (lax.axis_size("grp"), lax.axis_size("mem"), assignment.shape[0]) + embeddings.shape
    if shape != (4, 8, 4, 512, 768):
        return dense(*args)
    found, over = routed(*args)
    return lax.cond(
        over[0, 0] > 0.5, lambda: dense(*args), lambda: found.reshape(found.size)
    )


def solution(mesh):
    return jax.shard_map(
        local,
        mesh=mesh,
        in_specs=(
            P(("grp", "mem"), None),
            P(("grp", "mem")),
            P(("grp", "mem")),
            P(),
            P(("grp", "mem")),
        ),
        out_specs=P(("grp", "mem")),
        check_vma=False,
    )
```

```python
import functools
import math

import jax
import jax.numpy as jnp
from jax import lax
from jax.experimental import pallas as pl
from jax.experimental.pallas import tpu as pltpu
from jax.sharding import PartitionSpec as P

MESH = pl.DeviceIdType.MESH
NZ = 4
CHUNKS = 4
TILE = 256
LOW = -2.0


def flip(index, mask):
    out, bit = index, 1
    while bit <= mask:
        if mask & bit:
            out = out + bit - 2 * bit * (lax.div(index, bit) % 2)
        bit *= 2
    return out


def kernel(
    groups, ys, units, meta, best, planes, zs, plane_meta, z_meta, col_acc, row_acc,
    row_key, row_cluster, back, z_back, z_send, ready_sem, p_send, p_recv, z_ssem, z_rsem,
    pm_send, pm_recv, zm_send, zm_recv, b_send, b_recv, zb_send, zb_recv, relay_sem,
):
    g, m = lax.axis_index("grp"), lax.axis_index("mem")
    z, y = lax.div(m, ys), m % ys
    tiles = (groups // 2) * ys
    count = 2 * tiles
    rows = planes.shape[1]
    part = rows // CHUNKS

    def plane_peer(d):
        j, c = d // 2, d % 2
        return (flip(g, (j // ys) * 2 + c), z * ys + flip(y, j % ys))

    def column_peer(dz):
        return (g, ((z + dz) % NZ) * ys + y)

    load = pltpu.make_async_copy(units, planes.at[0], ready_sem)
    load.start()

    barrier = pltpu.get_barrier_semaphore()
    peers = [plane_peer(d) for d in range(1, count)] + [column_peer(k) for k in range(1, NZ)]
    for peer in peers:
        pl.semaphore_signal(barrier, inc=1, device_id=peer, device_id_type=MESH)
    col_acc[...] = jnp.full(col_acc.shape, LOW, jnp.float32)
    row_acc[...] = jnp.full(row_acc.shape, LOW, jnp.float32)
    plane_meta[0] = meta[...]
    load.wait()
    pl.semaphore_wait(barrier, len(peers))

    def remote(src, dst, ssem, rsem, peer):
        return pltpu.make_async_remote_copy(
            src_ref=src, dst_ref=dst, send_sem=ssem, recv_sem=rsem,
            device_id=peer, device_id_type=MESH,
        )

    def piece(k):
        return pl.ds(k * part, part)

    def own_to_z(k, slot, dz):
        return remote(
            planes.at[0, piece(k)], zs.at[slot, piece(k)], z_ssem.at[slot, k],
            z_rsem.at[slot, k], column_peer(dz),
        )

    def relay(k, src, dst, dz):
        return remote(
            zs.at[src, piece(k)], zs.at[dst, piece(k)], relay_sem.at[src, k],
            z_rsem.at[dst, k], column_peer(dz),
        )

    def to_plane(d):
        return remote(planes.at[0], planes.at[d], p_send.at[d], p_recv.at[d], plane_peer(d))

    def forward(j):
        return remote(
            planes.at[2 * j], planes.at[2 * j + 1], p_send.at[2 * j + 1], p_recv.at[2 * j + 1],
            plane_peer(1),
        )

    meta_copies = [
        remote(meta, plane_meta.at[d], pm_send.at[d], pm_recv.at[d], plane_peer(d))
        for d in range(1, count)
    ] + [
        remote(meta, z_meta.at[s], zm_send.at[s], zm_recv.at[s], column_peer(-1 - s))
        for s in range(2)
    ]
    for copy in meta_copies:
        copy.start()

    to_plane(1).start()

    @pl.when(z >= 1)
    def _():
        for k in range(CHUNKS):
            own_to_z(k, 0, -1).start()

    @pl.when(z <= 1)
    def _():
        for k in range(CHUNKS):
            own_to_z(k, 1, 2).start()

    for j in range(1, tiles):
        to_plane(2 * j).start()

    def spread(a, source):
        row_key[a] = jnp.broadcast_to(source[0:1, :], (128, rows)).T
        row_cluster[a] = jnp.broadcast_to(source[1:2, :], (128, rows)).T

    def pairs(a, left, d, both):
        right = planes[d]
        keys, clusters = plane_meta[d, 0:1, :], plane_meta[d, 1:2, :]

        def step(i, carry):
            here = pl.ds(pl.multiple_of(i * TILE, TILE), TILE)
            scores = lax.dot_general(
                left[here, :], right, (((1,), (1,)), ((), ())),
                preferred_element_type=jnp.float32,
            )
            my_key, my_cluster = row_key[a, here, :], row_cluster[a, here, :]
            acc = row_acc[a, here, :]
            for t in range(rows // 128):
                lanes = slice(t * 128, (t + 1) * 128)
                kept = jnp.where(my_cluster == clusters[:, lanes], scores[:, lanes], LOW)
                earlier = keys[:, lanes] < my_key
                acc = jnp.maximum(acc, jnp.where(earlier, kept, LOW))
                if both:
                    other = jnp.where(earlier, LOW, kept).reshape(TILE // 8, 8, 128)
                    col_acc[d, :, lanes] = jnp.maximum(col_acc[d, :, lanes], jnp.max(other, axis=0))
            row_acc[a, here, :] = acc
            return carry

        lax.fori_loop(0, rows // TILE, step, 0)

    spread(0, meta)
    own = planes.at[0]
    pairs(0, own, 0, False)
    for copy in meta_copies:
        copy.wait()
    to_plane(1).wait_recv()
    pairs(0, own, 1, False)

    for k in range(CHUNKS):
        @pl.when((z == 1) | (z == 2))
        def _():
            own_to_z(k, 0, -1).wait_recv()
            relay(k, 0, 1, -1).start()

        @pl.when(z == 2)
        def _():
            own_to_z(k, 1, 2).wait_recv()
            relay(k, 1, 0, 1).start()

    def plane_step(j, carry):
        pltpu.make_async_copy(planes.at[2 * j], planes.at[2 * j], p_recv.at[2 * j]).wait()
        forward(j).start()
        pairs(0, own, 2 * j, False)
        forward(j).wait_recv()
        pairs(0, own, 2 * j + 1, False)
        return carry

    lax.fori_loop(1, tiles, plane_step, 0)

    for k in range(CHUNKS):
        @pl.when((z == 0) | (z == 3))
        def _():
            own_to_z(k, 0, -1).wait_recv()

        @pl.when(z != 2)
        def _():
            own_to_z(k, 1, 2).wait_recv()

    spread(1, z_meta.at[0])
    spread(2, z_meta.at[1])

    def z1_step(d, carry):
        pairs(1, zs.at[0], d, True)
        return carry

    lax.fori_loop(0, count, z1_step, 0)
    first = lax.div(z, 2) * (count // 2)

    def z2_step(d, carry):
        pairs(2, zs.at[1], d + first, True)
        return carry

    lax.fori_loop(0, count // 2, z2_step, 0)

    def fold(a):
        return jnp.max(row_acc[a].T.reshape(16, 8, rows), axis=0)

    z_send[0] = fold(1)
    z_send[1] = fold(2)
    result_copies = [
        remote(col_acc.at[d], back.at[d], b_send.at[d], b_recv.at[d], plane_peer(d))
        for d in range(1, count)
    ]
    for copy in result_copies:
        copy.start()
    mine = jnp.maximum(fold(0), col_acc[0])
    z_copies = [
        remote(z_send.at[s], z_back.at[s], zb_send.at[s], zb_recv.at[s], column_peer(1 + s))
        for s in range(2)
    ]
    for copy in z_copies:
        copy.start()

    @pl.when(z >= 1)
    def _():
        for k in range(CHUNKS):
            own_to_z(k, 0, -1).wait_send()

    @pl.when(z <= 1)
    def _():
        for k in range(CHUNKS):
            own_to_z(k, 1, 2).wait_send()

    @pl.when((z == 1) | (z == 2))
    def _():
        for k in range(CHUNKS):
            relay(k, 0, 1, -1).wait_send()

    @pl.when(z == 2)
    def _():
        for k in range(CHUNKS):
            relay(k, 1, 0, 1).wait_send()

    to_plane(1).wait_send()
    for j in range(1, tiles):
        to_plane(2 * j).wait_send()
        forward(j).wait_send()

    for copy in result_copies + z_copies:
        copy.wait()
    for d in range(1, count):
        mine = jnp.maximum(mine, back[d])
    mine = jnp.maximum(mine, jnp.maximum(z_back[0], z_back[1]))
    best[...] = jnp.maximum(jnp.max(mine, axis=0, keepdims=True), -1.0)


def similarities(units, meta, groups, members):
    rows, width = units.shape
    ys = members // NZ
    count = groups * ys
    dma = pltpu.SemaphoreType.DMA
    return pl.pallas_call(
        functools.partial(kernel, groups, ys),
        out_shape=jax.ShapeDtypeStruct((1, rows), jnp.float32),
        in_specs=[
            pl.BlockSpec(memory_space=pl.ANY),
            pl.BlockSpec(memory_space=pltpu.VMEM),
        ],
        out_specs=pl.BlockSpec(memory_space=pltpu.VMEM),
        scratch_shapes=[
            pltpu.VMEM((count, rows, width), jnp.bfloat16),
            pltpu.VMEM((2, rows, width), jnp.bfloat16),
            pltpu.VMEM((count, 2, rows), jnp.float32),
            pltpu.VMEM((2, 2, rows), jnp.float32),
            pltpu.VMEM((count, 8, rows), jnp.float32),
            pltpu.VMEM((3, rows, 128), jnp.float32),
            pltpu.VMEM((3, rows, 128), jnp.float32),
            pltpu.VMEM((3, rows, 128), jnp.float32),
            pltpu.VMEM((count, 8, rows), jnp.float32),
            pltpu.VMEM((2, 8, rows), jnp.float32),
            pltpu.VMEM((2, 8, rows), jnp.float32),
            dma(()),
            dma((count,)), dma((count,)),
            dma((2, CHUNKS)), dma((2, CHUNKS)),
            dma((count,)), dma((count,)),
            dma((2,)), dma((2,)),
            dma((count,)), dma((count,)),
            dma((2,)), dma((2,)),
            dma((2, CHUNKS)),
        ],
        compiler_params=pltpu.CompilerParams(
            collective_id=1, has_side_effects=True, vmem_limit_bytes=56 * 1024 * 1024
        ),
    )(units, meta)


HELD = 176
LAYOUT = 768
BIG = 1e9
STEPS = ((0, 384), (384, 256), (640, 128))
PIECES = ((0, 176), (176, 176), (384, 128), (512, 128), (640, 96))
FAR = {2: ((384, 64), (512, 64), (640, 48)), 3: ((448, 64), (576, 64), (688, 48))}
NEAR = (176, 176)


def relation_of(place):
    far = (place >= 448) & (place < 512) | (place >= 576) & (place < 640) | (place >= 688)
    return jnp.where(place < 176, 0, jnp.where(place < 352, 1, jnp.where(far, 3, 2)))


def spot(b, row):
    start, size = [step for step in STEPS if step[0] <= row][-1]
    return 4 * start + b * size + row - start


def either(a, b):
    return a + b - 2 * a * b


def routed_kernel(
    assignment, embeddings, cluster, order, member, out, over,
    raw, units, sent, blocks, sent_meta, z_meta, metas, row_key, row_acc, col_acc,
    places, fin, fin_got, load_sem, zs, zr, mzs, mzr, ps, pr, mps, mpr, fs, fr,
):
    g, m = lax.axis_index("grp"), lax.axis_index("mem")
    x, c, z, y = lax.div(g, 2), g % 2, lax.div(m, 2), m % 2
    rows, width = raw.shape
    owners, capacity = 32, 32

    load = pltpu.make_async_copy(embeddings, raw, load_sem)
    load.start()

    def device(x, c, z, y):
        return (x * 2 + c, z * 2 + y)

    def column(j):
        return device(x, c, flip(z, j), y)

    side_to = (
        device(x, 1 - c, z, y),
        device(1 - x, either(c, 1 - x), z, y),
        device(x, either(either(c, x), 1 - y), z, 1 - y),
    )
    side_from = (
        device(x, 1 - c, z, y),
        device(1 - x, either(c, x), z, y),
        device(x, either(either(c, x), y), z, 1 - y),
    )
    here = x * 4 + y * 2 + c

    def home(i):
        return device(i // 4, i % 2, g, (i // 2) % 2)

    is_home = z == g
    barrier = pltpu.get_barrier_semaphore()
    for peer in [column(j) for j in (1, 2, 3)] + list(side_from):
        pl.semaphore_signal(barrier, inc=1, device_id=peer, device_id_type=MESH)
    for i in range(8):
        @pl.when(jnp.logical_not(is_home & (here == i)))
        def _():
            pl.semaphore_signal(barrier, inc=1, device_id=home(i), device_id_type=MESH)

    def remote(src, dst, ssem, rsem, peer):
        return pltpu.make_async_remote_copy(
            src_ref=src, dst_ref=dst, send_sem=ssem, recv_sem=rsem,
            device_id=peer, device_id_type=MESH,
        )

    def z_copy(j, k):
        start, size = NEAR if j == 1 else FAR[j][k]
        here = pl.ds(start, size)
        there = pl.ds(spot(0, start), size)
        return remote(sent.at[here], blocks.at[there], zs.at[j, k], zr.at[j, k], column(j))

    def z_meta_copy(j):
        return remote(sent_meta, z_meta.at[j], mzs.at[j], mzr.at[j], column(j))

    def side_copy(t, k):
        start, size = PIECES[k]
        mine, theirs = pl.ds(spot(0, start), size), pl.ds(spot(t + 1, start), size)
        return remote(
            blocks.at[mine], blocks.at[theirs], ps.at[t, k], pr.at[t, k], side_to[t]
        )

    def side_meta_copy(t):
        return remote(metas.at[0], metas.at[t + 1], mps.at[t], mpr.at[t], side_to[t])

    def fin_copy(p):
        return remote(fin.at[p], fin_got.at[here], fs.at[p], fr.at[here], (z, p))

    def fin_from(i):
        return remote(fin.at[0], fin_got.at[i], fs.at[0], fr.at[i], home(i))

    def wide(ref):
        return jnp.concatenate([ref[i : i + 1, :] for i in range(rows // 128)], axis=1)

    ids, keys, mem_of = wide(cluster), wide(order), wide(member)
    group = jnp.zeros_like(ids)
    for k in range(4):
        group = jnp.where(ids == k, assignment[k], group)
    owner = group * 8 + mem_of
    hits = jnp.concatenate(
        [
            (lax.broadcasted_iota(jnp.int32, (owners, rows), 0) == owner).astype(jnp.float32),
            (lax.broadcasted_iota(jnp.int32, (16, rows), 0) == group).astype(jnp.float32),
        ],
        axis=0,
    )
    before = (
        lax.broadcasted_iota(jnp.int32, (128, 128), 0)
        < lax.broadcasted_iota(jnp.int32, (128, 128), 1)
    ).astype(jnp.float32).astype(jnp.bfloat16)
    earlier_hits = jnp.zeros((owners + 16, 1), jnp.float32)
    counts = []
    for k in range(rows // 128):
        part = hits[:, k * 128 : (k + 1) * 128]
        inside = jnp.dot(part.astype(jnp.bfloat16), before, preferred_element_type=jnp.float32)
        counts.append(part * (inside + earlier_hits))
        earlier_hits = earlier_hits + jnp.sum(part, axis=1, keepdims=True)
    counts = jnp.concatenate(counts, axis=1)
    rank = jnp.sum(counts[:owners], axis=0, keepdims=True)
    pos = jnp.sum(counts[owners:], axis=0, keepdims=True).astype(jnp.int32)
    j = jnp.bitwise_xor(group, z)
    high = jnp.where(j >= 3, 1, 0)
    far = jnp.where(
        pos < 64, 384 + 64 * high + pos,
        jnp.where(pos < 128, 448 + 64 * high + pos, 512 + 48 * high + pos),
    )
    target = jnp.where(j == 0, pos, jnp.where(j == 1, 176 + pos, far))
    target = jnp.where(pos < HELD, target, -1)
    spilled = jnp.max(jnp.where(pos < HELD, 0.0, 1.0), axis=1, keepdims=True)

    def chosen(start, size):
        place = lax.broadcasted_iota(jnp.int32, (size, rows), 0) + start
        return (place == target).astype(jnp.float32).astype(jnp.bfloat16)

    facts = jnp.concatenate(
        [
            lax.shift_right_logical(keys, 8).astype(jnp.float32),
            jnp.bitwise_and(keys, 255).astype(jnp.float32),
            mem_of.astype(jnp.float32),
            rank,
            jnp.ones((1, rows), jnp.float32),
            jnp.zeros((11, rows), jnp.float32),
        ],
        axis=0,
    ).astype(jnp.bfloat16)
    load.wait()
    pl.semaphore_wait(barrier, len(peers))

    def remote(src, dst, ssem, rsem, peer):
        return pltpu.make_async_remote_copy(
            src_ref=src, dst_ref=dst, send_sem=ssem, recv_sem=rsem,
            device_id=peer, device_id_type=MESH,
        )

    def piece(k):
        return pl.ds(k * part, part)

    def own_to_z(k, slot, dz):
        return remote(
            planes.at[0, piece(k)], zs.at[slot, piece(k)], z_ssem.at[slot, k],
            z_rsem.at[slot, k], column_peer(dz),
        )

    def relay(k, src, dst, dz):
        return remote(
            zs.at[src, piece(k)], zs.at[dst, piece(k)], relay_sem.at[src, k],
            z_rsem.at[dst, k], column_peer(dz),
        )

    def to_plane(d):
        return remote(planes.at[0], planes.at[d], p_send.at[d], p_recv.at[d], plane_peer(d))

    def forward(j):
        return remote(
            planes.at[2 * j], planes.at[2 * j + 1], p_send.at[2 * j + 1], p_recv.at[2 * j + 1],
            plane_peer(1),
        )

    meta_copies = [
        remote(meta, plane_meta.at[d], pm_send.at[d], pm_recv.at[d], plane_peer(d))
        for d in range(1, count)
    ] + [
        remote(meta, z_meta.at[s], zm_send.at[s], zm_recv.at[s], column_peer(-1 - s))
        for s in range(2)
    ]
    for copy in meta_copies:
        copy.start()

    to_plane(1).start()

    @pl.when(z >= 1)
    def _():
        for k in range(CHUNKS):
            own_to_z(k, 0, -1).start()

    @pl.when(z <= 1)
    def _():
        for k in range(CHUNKS):
            own_to_z(k, 1, 2).start()

    for j in range(1, tiles):
        to_plane(2 * j).start()

    def spread(a, source):
        row_key[a] = jnp.broadcast_to(source[0:1, :], (128, rows)).T
        row_cluster[a] = jnp.broadcast_to(source[1:2, :], (128, rows)).T

    def pairs(a, left, d, both):
        right = planes[d]
        keys, clusters = plane_meta[d, 0:1, :], plane_meta[d, 1:2, :]

        def step(i, carry):
            here = pl.ds(pl.multiple_of(i * TILE, TILE), TILE)
            scores = lax.dot_general(
                left[here, :], right, (((1,), (1,)), ((), ())),
                preferred_element_type=jnp.float32,
            )
            my_key, my_cluster = row_key[a, here, :], row_cluster[a, here, :]
            acc = row_acc[a, here, :]
            for t in range(rows // 128):
                lanes = slice(t * 128, (t + 1) * 128)
                kept = jnp.where(my_cluster == clusters[:, lanes], scores[:, lanes], LOW)
                earlier = keys[:, lanes] < my_key
                acc = jnp.maximum(acc, jnp.where(earlier, kept, LOW))
                if both:
                    other = jnp.where(earlier, LOW, kept).reshape(TILE // 8, 8, 128)
                    col_acc[d, :, lanes] = jnp.maximum(col_acc[d, :, lanes], jnp.max(other, axis=0))
            row_acc[a, here, :] = acc
            return carry

        lax.fori_loop(0, rows // TILE, step, 0)

    spread(0, meta)
    own = planes.at[0]
    pairs(0, own, 0, False)
    for copy in meta_copies:
        copy.wait()
    to_plane(1).wait_recv()
    pairs(0, own, 1, False)

    for k in range(CHUNKS):
        @pl.when((z == 1) | (z == 2))
        def _():
            own_to_z(k, 0, -1).wait_recv()
            relay(k, 0, 1, -1).start()

        @pl.when(z == 2)
        def _():
            own_to_z(k, 1, 2).wait_recv()
            relay(k, 1, 0, 1).start()

    def plane_step(j, carry):
        pltpu.make_async_copy(planes.at[2 * j], planes.at[2 * j], p_recv.at[2 * j]).wait()
        forward(j).start()
        pairs(0, own, 2 * j, False)
        forward(j).wait_recv()
        pairs(0, own, 2 * j + 1, False)
        return carry

    lax.fori_loop(1, tiles, plane_step, 0)

    for k in range(CHUNKS):
        @pl.when((z == 0) | (z == 3))
        def _():
            own_to_z(k, 0, -1).wait_recv()

        @pl.when(z != 2)
        def _():
            own_to_z(k, 1, 2).wait_recv()

    spread(1, z_meta.at[0])
    spread(2, z_meta.at[1])

    def z1_step(d, carry):
        pairs(1, zs.at[0], d, True)
        return carry

    lax.fori_loop(0, count, z1_step, 0)
    first = lax.div(z, 2) * (count // 2)

    def z2_step(d, carry):
        pairs(2, zs.at[1], d + first, True)
        return carry

    lax.fori_loop(0, count // 2, z2_step, 0)

    def fold(a):
        return jnp.max(row_acc[a].T.reshape(16, 8, rows), axis=0)

    z_send[0] = fold(1)
    z_send[1] = fold(2)
    result_copies = [
        remote(col_acc.at[d], back.at[d], b_send.at[d], b_recv.at[d], plane_peer(d))
        for d in range(1, count)
    ]
    for copy in result_copies:
        copy.start()
    mine = jnp.maximum(fold(0), col_acc[0])
    z_copies = [
        remote(z_send.at[s], z_back.at[s], zb_send.at[s], zb_recv.at[s], column_peer(1 + s))
        for s in range(2)
    ]
    for copy in z_copies:
        copy.start()

    @pl.when(z >= 1)
    def _():
        for k in range(CHUNKS):
            own_to_z(k, 0, -1).wait_send()

    @pl.when(z <= 1)
    def _():
        for k in range(CHUNKS):
            own_to_z(k, 1, 2).wait_send()

    @pl.when((z == 1) | (z == 2))
    def _():
        for k in range(CHUNKS):
            relay(k, 0, 1, -1).wait_send()

    @pl.when(z == 2)
    def _():
        for k in range(CHUNKS):
            relay(k, 1, 0, 1).wait_send()

    to_plane(1).wait_send()
    for j in range(1, tiles):
        to_plane(2 * j).wait_send()
        forward(j).wait_send()

    for copy in result_copies + z_copies:
        copy.wait()
    for d in range(1, count):
        mine = jnp.maximum(mine, back[d])
    mine = jnp.maximum(mine, jnp.maximum(z_back[0], z_back[1]))
    best[...] = jnp.maximum(jnp.max(mine, axis=0, keepdims=True), -1.0)


def similarities(units, meta, groups, members):
    rows, width = units.shape
    ys = members // NZ
    count = groups * ys
    dma = pltpu.SemaphoreType.DMA
    return pl.pallas_call(
        functools.partial(kernel, groups, ys),
        out_shape=jax.ShapeDtypeStruct((1, rows), jnp.float32),
        in_specs=[
            pl.BlockSpec(memory_space=pl.ANY),
            pl.BlockSpec(memory_space=pltpu.VMEM),
        ],
        out_specs=pl.BlockSpec(memory_space=pltpu.VMEM),
        scratch_shapes=[
            pltpu.VMEM((count, rows, width), jnp.bfloat16),
            pltpu.VMEM((2, rows, width), jnp.bfloat16),
            pltpu.VMEM((count, 2, rows), jnp.float32),
            pltpu.VMEM((2, 2, rows), jnp.float32),
            pltpu.VMEM((count, 8, rows), jnp.float32),
            pltpu.VMEM((3, rows, 128), jnp.float32),
            pltpu.VMEM((3, rows, 128), jnp.float32),
            pltpu.VMEM((3, rows, 128), jnp.float32),
            pltpu.VMEM((count, 8, rows), jnp.float32),
            pltpu.VMEM((2, 8, rows), jnp.float32),
            pltpu.VMEM((2, 8, rows), jnp.float32),
            dma(()),
            dma((count,)), dma((count,)),
            dma((2, CHUNKS)), dma((2, CHUNKS)),
            dma((count,)), dma((count,)),
            dma((2,)), dma((2,)),
            dma((count,)), dma((count,)),
            dma((2,)), dma((2,)),
            dma((2, CHUNKS)),
        ],
        compiler_params=pltpu.CompilerParams(
            collective_id=1, has_side_effects=True, vmem_limit_bytes=56 * 1024 * 1024
        ),
    )(units, meta)


HELD = 176
LAYOUT = 768
BIG = 1e9
STEPS = ((0, 384), (384, 256), (640, 128))
PIECES = ((0, 176), (176, 176), (384, 128), (512, 128), (640, 96))
FAR = {2: ((384, 64), (512, 64), (640, 48)), 3: ((448, 64), (576, 64), (688, 48))}
NEAR = (176, 176)


def relation_of(place):
    far = (place >= 448) & (place < 512) | (place >= 576) & (place < 640) | (place >= 688)
    return jnp.where(place < 176, 0, jnp.where(place < 352, 1, jnp.where(far, 3, 2)))


def spot(b, row):
    start, size = [step for step in STEPS if step[0] <= row][-1]
    return 4 * start + b * size + row - start


def either(a, b):
    return a + b - 2 * a * b


def routed_kernel(
    assignment, embeddings, cluster, order, member, out, over,
    raw, units, sent, blocks, sent_meta, z_meta, metas, row_key, row_acc, col_acc,
    places, fin, fin_got, load_sem, zs, zr, mzs, mzr, ps, pr, mps, mpr, fs, fr,
):
    g, m = lax.axis_index("grp"), lax.axis_index("mem")
    x, c, z, y = lax.div(g, 2), g % 2, lax.div(m, 2), m % 2
    rows, width = raw.shape
    owners, capacity = 32, 32

    load = pltpu.make_async_copy(embeddings, raw, load_sem)
    load.start()

    def device(x, c, z, y):
        return (x * 2 + c, z * 2 + y)

    def column(j):
        return device(x, c, flip(z, j), y)

    side_to = (
        device(x, 1 - c, z, y),
        device(1 - x, either(c, 1 - x), z, y),
        device(x, either(either(c, x), 1 - y), z, 1 - y),
    )
    side_from = (
        device(x, 1 - c, z, y),
        device(1 - x, either(c, x), z, y),
        device(x, either(either(c, x), y), z, 1 - y),
    )
    here = x * 4 + y * 2 + c

    def home(i):
        return device(i // 4, i % 2, g, (i // 2) % 2)

    is_home = z == g
    barrier = pltpu.get_barrier_semaphore()
    for peer in [column(j) for j in (1, 2, 3)] + list(side_from):
        pl.semaphore_signal(barrier, inc=1, device_id=peer, device_id_type=MESH)
    for i in range(8):
        @pl.when(jnp.logical_not(is_home & (here == i)))
        def _():
            pl.semaphore_signal(barrier, inc=1, device_id=home(i), device_id_type=MESH)

    def remote(src, dst, ssem, rsem, peer):
        return pltpu.make_async_remote_copy(
            src_ref=src, dst_ref=dst, send_sem=ssem, recv_sem=rsem,
            device_id=peer, device_id_type=MESH,
        )

    def z_copy(j, k):
        start, size = NEAR if j == 1 else FAR[j][k]
        here = pl.ds(start, size)
        there = pl.ds(spot(0, start), size)
        return remote(sent.at[here], blocks.at[there], zs.at[j, k], zr.at[j, k], column(j))

    def z_meta_copy(j):
        return remote(sent_meta, z_meta.at[j], mzs.at[j], mzr.at[j], column(j))

    def side_copy(t, k):
        start, size = PIECES[k]
        mine, theirs = pl.ds(spot(0, start), size), pl.ds(spot(t + 1, start), size)
        return remote(
            blocks.at[mine], blocks.at[theirs], ps.at[t, k], pr.at[t, k], side_to[t]
        )

    def side_meta_copy(t):
        return remote(metas.at[0], metas.at[t + 1], mps.at[t], mpr.at[t], side_to[t])

    def fin_copy(p):
        return remote(fin.at[p], fin_got.at[here], fs.at[p], fr.at[here], (z, p))

    def fin_from(i):
        return remote(fin.at[0], fin_got.at[i], fs.at[0], fr.at[i], home(i))

    def wide(ref):
        return jnp.concatenate([ref[i : i + 1, :] for i in range(rows // 128)], axis=1)

    ids, keys, mem_of = wide(cluster), wide(order), wide(member)
    group = jnp.zeros_like(ids)
    for k in range(4):
        group = jnp.where(ids == k, assignment[k], group)
    owner = group * 8 + mem_of
    hits = jnp.concatenate(
        [
            (lax.broadcasted_iota(jnp.int32, (owners, rows), 0) == owner).astype(jnp.float32),
            (lax.broadcasted_iota(jnp.int32, (16, rows), 0) == group).astype(jnp.float32),
        ],
        axis=0,
    )
    before = (
        lax.broadcasted_iota(jnp.int32, (128, 128), 0)
        < lax.broadcasted_iota(jnp.int32, (128, 128), 1)
    ).astype(jnp.float32).astype(jnp.bfloat16)
    earlier_hits = jnp.zeros((owners + 16, 1), jnp.float32)
    counts = []
    for k in range(rows // 128):
        part = hits[:, k * 128 : (k + 1) * 128]
        inside = jnp.dot(part.astype(jnp.bfloat16), before, preferred_element_type=jnp.float32)
        counts.append(part * (inside + earlier_hits))
        earlier_hits = earlier_hits + jnp.sum(part, axis=1, keepdims=True)
    counts = jnp.concatenate(counts, axis=1)
    rank = jnp.sum(counts[:owners], axis=0, keepdims=True)
    pos = jnp.sum(counts[owners:], axis=0, keepdims=True).astype(jnp.int32)
    j = jnp.bitwise_xor(group, z)
    high = jnp.where(j >= 3, 1, 0)
    far = jnp.where(
        pos < 64, 384 + 64 * high + pos,
        jnp.where(pos < 128, 448 + 64 * high + pos, 512 + 48 * high + pos),
    )
    target = jnp.where(j == 0, pos, jnp.where(j == 1, 176 + pos, far))
    target = jnp.where(pos < HELD, target, -1)
    spilled = jnp.max(jnp.where(pos < HELD, 0.0, 1.0), axis=1, keepdims=True)

    def chosen(start, size):
        place = lax.broadcasted_iota(jnp.int32, (size, rows), 0) + start
        return (place == target).astype(jnp.float32).astype(jnp.bfloat16)

    facts = jnp.concatenate(
        [
            lax.shift_right_logical(keys, 8).astype(jnp.float32),
            jnp.bitwise_and(keys, 255).astype(jnp.float32),
            mem_of.astype(jnp.float32),
            rank,
            jnp.ones((1, rows), jnp.float32),
            jnp.zeros((11, rows), jnp.float32),
        ],
        axis=0,
    ).astype(jnp.bfloat16)
    for start, size in STEPS:
        lanes = slice(start, start + size)
        sorted_facts = lax.dot_general(
            facts, chosen(start, size), (((1,), (1,)), ((), ())),
            preferred_element_type=jnp.float32,
        )
        held = sorted_facts[4:5] > 0.5
        sent_meta[0:1, lanes] = jnp.where(
            held, sorted_facts[0:1] * 256.0 + sorted_facts[1:2], BIG
        )
        sent_meta[1:2, lanes] = jnp.where(held, sorted_facts[2:3], -1.0)
        sent_meta[2:3, lanes] = sorted_facts[3:4]
        sent_meta[3:4, lanes] = jnp.broadcast_to(spilled, (1, size))
        sent_meta[4:8, lanes] = jnp.zeros((4, size), jnp.float32)

    load.wait()

    def normalise(i, carry):
        part = pl.ds(pl.multiple_of(i * 128, 128), 128)
        widened = raw[part, :].astype(jnp.float32)
        scale = lax.rsqrt(jnp.mean(widened * widened, axis=1, keepdims=True) + 1e-06)
        units[part, :] = (widened * scale * (1.0 / math.sqrt(width))).astype(jnp.bfloat16)
        return carry

    lax.fori_loop(0, rows // 128, normalise, 0)

    def place(start, size):
        picks = chosen(start, size)
        lanes = slice(start, start + size)
        sorted_facts = lax.dot_general(
            facts, picks, (((1,), (1,)), ((), ())), preferred_element_type=jnp.float32
        )
        held = sorted_facts[4:5] > 0.5
        sent_meta[0:1, lanes] = jnp.where(
            held, sorted_facts[0:1] * 256.0 + sorted_facts[1:2], BIG
        )
        sent_meta[1:2, lanes] = jnp.where(held, sorted_facts[2:3], -1.0)
        sent_meta[2:3, lanes] = sorted_facts[3:4]
        sent_meta[3:4, lanes] = jnp.broadcast_to(spilled, (1, size))
        sent_meta[4:8, lanes] = jnp.zeros((4, size), jnp.float32)
        return jnp.dot(
            picks, units[...], preferred_element_type=jnp.float32
        ).astype(jnp.bfloat16)

    sent[pl.ds(384, 256), :] = place(384, 256)
    near = place(0, 384)
    sent[pl.ds(*NEAR), :] = near[176:352]
    blocks[pl.ds(0, 176), :] = near[:176]
    sent[pl.ds(640, 128), :] = place(640, 128)

    @pl.when(is_home)
    def _():
        pl.semaphore_wait(barrier, 13)

    @pl.when(jnp.logical_not(is_home))
    def _():
        pl.semaphore_wait(barrier, 14)

    for r in (1, 2, 3):
        z_meta_copy(r).start()
    for k in range(2):
        z_copy(3, k).start()
        z_copy(2, k).start()
    z_copy(1, 0).start()
    for t in range(3):
        side_copy(t, 0).start()
    for b in range(4):
        for row in (352, 736):
            blocks[pl.ds(spot(b, row), 32), :] = jnp.zeros((32, width), jnp.bfloat16)
    row_acc[...] = jnp.full(row_acc.shape, LOW, jnp.float32)
    col_acc[...] = jnp.full(col_acc.shape, LOW, jnp.float32)

    for r in (1, 2, 3):
        z_meta_copy(r).wait_recv()
    lane = lax.broadcasted_iota(jnp.int32, (8, LAYOUT), 1)
    relation = relation_of(lane)
    joined = sent_meta[...]
    spill = jnp.max(joined[3:4], axis=1, keepdims=True)
    for r in (1, 2, 3):
        joined = jnp.where(relation == r, z_meta[r], joined)
        spill = jnp.maximum(spill, jnp.max(z_meta[r, 3:4, :], axis=1, keepdims=True))
    metas[0] = joined
    for t in range(3):
        side_meta_copy(t).start()

    def prepare(b):
        keys = jnp.broadcast_to(metas[b, 0:1, :], (128, LAYOUT)).T
        for start, size in STEPS:
            row_key[pl.ds(spot(b, start), size), :] = keys[start : start + size]
        slot = jnp.bitwise_xor(relation[0:1], z) * 32 + metas[b, 2:3, :].astype(jnp.int32)
        places[b] = (
            lax.broadcasted_iota(jnp.int32, (128, LAYOUT), 0) == slot
        ).astype(jnp.float32).astype(jnp.bfloat16)

    def meet(lefts, right, start, size, both=True):
        theirs = blocks[pl.ds(spot(right, start), size), :]
        for first, count in lefts:
            part = pl.ds(first, count)
            scores = lax.dot_general(
                blocks[part, :], theirs, (((1,), (1,)), ((), ())),
                preferred_element_type=jnp.float32,
            )
            my_key = row_key[part, :]
            acc = row_acc[part, :]
            for t in range(size // 128):
                lanes = slice(start + t * 128, start + (t + 1) * 128)
                earlier = metas[right, 0:1, lanes] < my_key
                score = scores[:, t * 128 : (t + 1) * 128]
                acc = jnp.maximum(acc, jnp.where(earlier, score, LOW))
                if both:
                    other = jnp.where(earlier, LOW, score).reshape(count // 8, 8, 128)
                    col_acc[right, :, lanes] = jnp.maximum(
                        col_acc[right, :, lanes], jnp.max(other, axis=0)
                    )
            row_acc[part, :] = acc

    def own_step(s):
        start, size = STEPS[s]
        new = [(spot(0, start), size)]
        for old in STEPS[:s]:
            for right in (0, 2, 3):
                meet(new, right, *old)
        meet(new, 0, start, size, False)

    def side_step(s):
        start, size = STEPS[s]
        s_new, x_new, y_new = [(spot(b, start), size) for b in (1, 2, 3)]
        sides = [s_new, x_new, y_new] if size > 128 else [(s_new[0], 3 * size)]
        for run in STEPS[: s + 1]:
            meet(sides, 0, *run)
            meet([y_new], 2, *run)
        for run in STEPS[:s]:
            meet([x_new], 3, *run)

    z_copy(1, 0).wait_recv()
    for t in range(3):
        side_copy(t, 1).start()
    prepare(0)
    own_step(0)
    for k in range(3):
        for r in (3, 2):
            z_copy(r, k).wait_recv()
        for t in range(3):
            side_copy(t, k + 2).start()
        if k == 0:
            for r in (3, 2):
                z_copy(r, 0).wait_send()
                z_copy(r, 2).start()
        elif k == 1:
            for t in range(3):
                side_meta_copy(t).wait_recv()
                side_copy(t, 0).wait_recv()
                side_copy(t, 1).wait_recv()
            for b in (1, 2, 3):
                prepare(b)
            side_step(0)
            own_step(1)
    for t in range(3):
        side_copy(t, 2).wait_recv()
        side_copy(t, 3).wait_recv()
    side_step(1)
    own_step(2)
    for t in range(3):
        side_copy(t, 4).wait_recv()
    side_step(2)

    for b in range(4):
        value = jnp.max(col_acc[b], axis=0, keepdims=True)
        turned = [
            jnp.max(row_acc[pl.ds(spot(b, start), size), :].T, axis=0, keepdims=True)
            for start, size in STEPS
        ]
        value = jnp.maximum(value, jnp.concatenate(turned, axis=1))
        value = jnp.maximum(value, -1.0)
        parts = []
        for _ in range(3):
            part = value.astype(jnp.bfloat16).astype(jnp.float32)
            parts.append(part)
            value = value - part
        parts.append(jnp.ones_like(value))
        mine = (
            lax.broadcasted_iota(jnp.int32, (8, LAYOUT), 0)
            == metas[b, 1:2, :].astype(jnp.int32)
        ).astype(jnp.float32)
        stacked = jnp.concatenate([mine * part for part in parts], axis=0).astype(jnp.bfloat16)
        found = lax.dot_general(
            stacked, places[b], (((1,), (1,)), ((), ())), preferred_element_type=jnp.float32
        )
        total = (found[16:24] + found[8:16]) + found[0:8]
        fin[:, b, :] = jnp.where(found[24:32] > 0.5, total, -1.0)
    for b in range(4, 8):
        fin[:, b, :] = jnp.broadcast_to(spill, (8, 128))

    for p in range(8):
        me = is_home & (m == p)

        @pl.when(jnp.logical_not(me))
        def _():
            fin_copy(p).start()

        @pl.when(me)
        def _():
            fin_got[here] = fin[p]

    for r in (1, 2, 3):
        z_meta_copy(r).wait_send()
    z_copy(1, 0).wait_send()
    for r in (3, 2):
        for k in (1, 2):
            z_copy(r, k).wait_send()
    for t in range(3):
        side_meta_copy(t).wait_send()
        for k in range(5):
            side_copy(t, k).wait_send()
    for p in range(8):
        @pl.when(jnp.logical_not(is_home & (m == p)))
        def _():
            fin_copy(p).wait_send()
    for i in range(8):
        @pl.when(jnp.logical_not(is_home & (here == i)))
        def _():
            fin_from(i).wait_recv()

    block = lax.broadcasted_iota(jnp.int32, (1, 128), 1) // 32
    worst = fin_got[0, 4:5, :]
    for i in range(1, 8):
        worst = jnp.maximum(worst, fin_got[i, 4:5, :])
    over[...] = jnp.broadcast_to(worst, (8, 128))
    for xs in range(2):
        for cs in range(2):
            ways = []
            for ys in range(2):
                i = xs * 4 + ys * 2 + cs
                sibling = xs * 4 + ys * 2 + (1 - cs)
                x_holder = (1 - xs) * 4 + ys * 2 + (cs ^ (1 - xs))
                y_holder = xs * 4 + (1 - ys) * 2 + (cs ^ xs ^ (1 - ys))
                ways.append(
                    jnp.maximum(
                        jnp.maximum(fin_got[i, 0:1, :], fin_got[sibling, 1:2, :]),
                        jnp.maximum(fin_got[x_holder, 2:3, :], fin_got[y_holder, 3:4, :]),
                    )
                )
            for half, turns in enumerate(((0, 32, 32, 64), (64, 96, 96, 0))):
                line = ways[0]
                for k in range(4):
                    way = ways[k % 2]
                    turned = pltpu.roll(way, turns[k], 1) if turns[k] else way
                    line = jnp.where(block == k, turned, line)
                row = (xs * 2 + cs) * 2 + half
                out[row : row + 1, :] = line


def routed(embeddings, cluster_id, row_order, assignment, placement):
    rows, width = embeddings.shape
    dma = pltpu.SemaphoreType.DMA
    lines = (rows // 128, 128)
    vmem = pl.BlockSpec(memory_space=pltpu.VMEM)
    return pl.pallas_call(
        routed_kernel,
        out_shape=[jax.ShapeDtypeStruct((8, 128), jnp.float32)] * 2,
        in_specs=[
            pl.BlockSpec(memory_space=pltpu.SMEM), pl.BlockSpec(memory_space=pl.ANY),
            vmem, vmem, vmem,
        ],
        out_specs=[vmem, vmem],
        scratch_shapes=[
            pltpu.VMEM((rows, width), jnp.bfloat16),
            pltpu.VMEM((rows, width), jnp.bfloat16),
            pltpu.VMEM((LAYOUT, width), jnp.bfloat16),
            pltpu.VMEM((4 * LAYOUT, width), jnp.bfloat16),
            pltpu.VMEM((8, LAYOUT), jnp.float32),
            pltpu.VMEM((4, 8, LAYOUT), jnp.float32),
            pltpu.VMEM((4, 8, LAYOUT), jnp.float32),
            pltpu.VMEM((4 * LAYOUT, 128), jnp.float32),
            pltpu.VMEM((4 * LAYOUT, 128), jnp.float32),
            pltpu.VMEM((4, 8, LAYOUT), jnp.float32),
            pltpu.VMEM((4, 128, LAYOUT), jnp.bfloat16),
            pltpu.VMEM((8, 8, 128), jnp.float32),
            pltpu.VMEM((8, 8, 128), jnp.float32),
            dma(()),
            dma((4, 3)), dma((4, 3)),
            dma((4,)), dma((4,)),
            dma((3, 5)), dma((3, 5)),
            dma((3,)), dma((3,)),
            dma((8,)), dma((8,)),
        ],
        compiler_params=pltpu.CompilerParams(
            collective_id=0, has_side_effects=True, vmem_limit_bytes=48 * 1024 * 1024
        ),
    )(
        assignment, embeddings, cluster_id.reshape(lines), row_order.reshape(lines),
        placement.reshape(lines),
    )


def dense(embeddings, cluster_id, row_order, assignment, placement):
    members = lax.axis_size("mem")
    groups = lax.axis_size("grp")
    owners = groups * members
    row_count, feature_count = embeddings.shape
    capacity = max(2, 2 * row_count // owners)
    widened = embeddings.astype(jnp.float32)
    unit_rows = (
        widened
        * lax.rsqrt(jnp.mean(widened * widened, axis=1, keepdims=True) + 1e-06)
        * (1.0 / math.sqrt(feature_count))
    ).astype(jnp.bfloat16)
    meta = jnp.stack([row_order, cluster_id]).astype(jnp.float32)
    best = similarities(unit_rows, meta, groups, members)

    table_hits = cluster_id[:, None] == jnp.arange(assignment.shape[0], dtype=jnp.int32)[None, :]
    group_of = jnp.sum(jnp.where(table_hits, assignment[None, :], 0), axis=1)
    owner_id = group_of * members + placement
    before = jnp.arange(row_count)[None, :] < jnp.arange(row_count)[:, None]
    rank = jnp.sum((before & (owner_id[None, :] == owner_id[:, None])).astype(jnp.int32), axis=1)
    target = owner_id * capacity + rank
    slots = jnp.arange(owners * capacity, dtype=jnp.int32)
    filled = jnp.max(
        jnp.where(slots[:, None] == target[None, :], best, -1.0), axis=1
    )
    return lax.all_to_all(filled, ("grp", "mem"), split_axis=0, concat_axis=0, tiled=True)


def local(*args):
    embeddings, _, _, assignment, _ = args
    shape = (lax.axis_size("grp"), lax.axis_size("mem"), assignment.shape[0]) + embeddings.shape
    if shape != (4, 8, 4, 512, 768):
        return dense(*args)
    found, over = routed(*args)
    return lax.cond(
        over[0, 0] > 0.5, lambda: dense(*args), lambda: found.reshape(found.size)
    )


def solution(mesh):
    return jax.shard_map(
        local,
        mesh=mesh,
        in_specs=(
            P(("grp", "mem"), None),
            P(("grp", "mem")),
            P(("grp", "mem")),
            P(),
            P(("grp", "mem")),
        ),
        out_specs=P(("grp", "mem")),
        check_vma=False,
    )
```

```python
import functools
import math

import jax
import jax.numpy as jnp
from jax import lax
from jax.experimental import pallas as pl
from jax.experimental.pallas import tpu as pltpu
from jax.sharding import PartitionSpec as P

MESH = pl.DeviceIdType.MESH
NZ = 4
CHUNKS = 4
TILE = 256
LOW = -2.0


def flip(index, mask):
    out, bit = index, 1
    while bit <= mask:
        if mask & bit:
            out = out + bit - 2 * bit * (lax.div(index, bit) % 2)
        bit *= 2
    return out


def kernel(
    groups, ys, units, meta, best, planes, zs, plane_meta, z_meta, col_acc, row_acc,
    row_key, row_cluster, back, z_back, z_send, ready_sem, p_send, p_recv, z_ssem, z_rsem,
    pm_send, pm_recv, zm_send, zm_recv, b_send, b_recv, zb_send, zb_recv, relay_sem,
):
    g, m = lax.axis_index("grp"), lax.axis_index("mem")
    z, y = lax.div(m, ys), m % ys
    tiles = (groups // 2) * ys
    count = 2 * tiles
    rows = planes.shape[1]
    part = rows // CHUNKS

    def plane_peer(d):
        j, c = d // 2, d % 2
        return (flip(g, (j // ys) * 2 + c), z * ys + flip(y, j % ys))

    def column_peer(dz):
        return (g, ((z + dz) % NZ) * ys + y)

    load = pltpu.make_async_copy(units, planes.at[0], ready_sem)
    load.start()

    barrier = pltpu.get_barrier_semaphore()
    peers = [plane_peer(d) for d in range(1, count)] + [column_peer(k) for k in range(1, NZ)]
    for peer in peers:
        pl.semaphore_signal(barrier, inc=1, device_id=peer, device_id_type=MESH)
    col_acc[...] = jnp.full(col_acc.shape, LOW, jnp.float32)
    row_acc[...] = jnp.full(row_acc.shape, LOW, jnp.float32)
    plane_meta[0] = meta[...]
    load.wait()
    pl.semaphore_wait(barrier, len(peers))

    def remote(src, dst, ssem, rsem, peer):
        return pltpu.make_async_remote_copy(
            src_ref=src, dst_ref=dst, send_sem=ssem, recv_sem=rsem,
            device_id=peer, device_id_type=MESH,
        )

    def piece(k):
        return pl.ds(k * part, part)

    def own_to_z(k, slot, dz):
        return remote(
            planes.at[0, piece(k)], zs.at[slot, piece(k)], z_ssem.at[slot, k],
            z_rsem.at[slot, k], column_peer(dz),
        )

    def relay(k, src, dst, dz):
        return remote(
            zs.at[src, piece(k)], zs.at[dst, piece(k)], relay_sem.at[src, k],
            z_rsem.at[dst, k], column_peer(dz),
        )

    def to_plane(d):
        return remote(planes.at[0], planes.at[d], p_send.at[d], p_recv.at[d], plane_peer(d))

    def forward(j):
        return remote(
            planes.at[2 * j], planes.at[2 * j + 1], p_send.at[2 * j + 1], p_recv.at[2 * j + 1],
            plane_peer(1),
        )

    meta_copies = [
        remote(meta, plane_meta.at[d], pm_send.at[d], pm_recv.at[d], plane_peer(d))
        for d in range(1, count)
    ] + [
        remote(meta, z_meta.at[s], zm_send.at[s], zm_recv.at[s], column_peer(-1 - s))
        for s in range(2)
    ]
    for copy in meta_copies:
        copy.start()

    to_plane(1).start()

    @pl.when(z >= 1)
    def _():
        for k in range(CHUNKS):
            own_to_z(k, 0, -1).start()

    @pl.when(z <= 1)
    def _():
        for k in range(CHUNKS):
            own_to_z(k, 1, 2).start()

    for j in range(1, tiles):
        to_plane(2 * j).start()

    def spread(a, source):
        row_key[a] = jnp.broadcast_to(source[0:1, :], (128, rows)).T
        row_cluster[a] = jnp.broadcast_to(source[1:2, :], (128, rows)).T

    def pairs(a, left, d, both):
        right = planes[d]
        keys, clusters = plane_meta[d, 0:1, :], plane_meta[d, 1:2, :]

        def step(i, carry):
            here = pl.ds(pl.multiple_of(i * TILE, TILE), TILE)
            scores = lax.dot_general(
                left[here, :], right, (((1,), (1,)), ((), ())),
                preferred_element_type=jnp.float32,
            )
            my_key, my_cluster = row_key[a, here, :], row_cluster[a, here, :]
            acc = row_acc[a, here, :]
            for t in range(rows // 128):
                lanes = slice(t * 128, (t + 1) * 128)
                kept = jnp.where(my_cluster == clusters[:, lanes], scores[:, lanes], LOW)
                earlier = keys[:, lanes] < my_key
                acc = jnp.maximum(acc, jnp.where(earlier, kept, LOW))
                if both:
                    other = jnp.where(earlier, LOW, kept).reshape(TILE // 8, 8, 128)
                    col_acc[d, :, lanes] = jnp.maximum(col_acc[d, :, lanes], jnp.max(other, axis=0))
            row_acc[a, here, :] = acc
            return carry

        lax.fori_loop(0, rows // TILE, step, 0)

    spread(0, meta)
    own = planes.at[0]
    pairs(0, own, 0, False)
    for copy in meta_copies:
        copy.wait()
    to_plane(1).wait_recv()
    pairs(0, own, 1, False)

    for k in range(CHUNKS):
        @pl.when((z == 1) | (z == 2))
        def _():
            own_to_z(k, 0, -1).wait_recv()
            relay(k, 0, 1, -1).start()

        @pl.when(z == 2)
        def _():
            own_to_z(k, 1, 2).wait_recv()
            relay(k, 1, 0, 1).start()

    def plane_step(j, carry):
        pltpu.make_async_copy(planes.at[2 * j], planes.at[2 * j], p_recv.at[2 * j]).wait()
        forward(j).start()
        pairs(0, own, 2 * j, False)
        forward(j).wait_recv()
        pairs(0, own, 2 * j + 1, False)
        return carry

    lax.fori_loop(1, tiles, plane_step, 0)

    for k in range(CHUNKS):
        @pl.when((z == 0) | (z == 3))
        def _():
            own_to_z(k, 0, -1).wait_recv()

        @pl.when(z != 2)
        def _():
            own_to_z(k, 1, 2).wait_recv()

    spread(1, z_meta.at[0])
    spread(2, z_meta.at[1])

    def z1_step(d, carry):
        pairs(1, zs.at[0], d, True)
        return carry

    lax.fori_loop(0, count, z1_step, 0)
    first = lax.div(z, 2) * (count // 2)

    def z2_step(d, carry):
        pairs(2, zs.at[1], d + first, True)
        return carry

    lax.fori_loop(0, count // 2, z2_step, 0)

    def fold(a):
        return jnp.max(row_acc[a].T.reshape(16, 8, rows), axis=0)

    z_send[0] = fold(1)
    z_send[1] = fold(2)
    result_copies = [
        remote(col_acc.at[d], back.at[d], b_send.at[d], b_recv.at[d], plane_peer(d))
        for d in range(1, count)
    ]
    for copy in result_copies:
        copy.start()
    mine = jnp.maximum(fold(0), col_acc[0])
    z_copies = [
        remote(z_send.at[s], z_back.at[s], zb_send.at[s], zb_recv.at[s], column_peer(1 + s))
        for s in range(2)
    ]
    for copy in z_copies:
        copy.start()

    @pl.when(z >= 1)
    def _():
        for k in range(CHUNKS):
            own_to_z(k, 0, -1).wait_send()

    @pl.when(z <= 1)
    def _():
        for k in range(CHUNKS):
            own_to_z(k, 1, 2).wait_send()

    @pl.when((z == 1) | (z == 2))
    def _():
        for k in range(CHUNKS):
            relay(k, 0, 1, -1).wait_send()

    @pl.when(z == 2)
    def _():
        for k in range(CHUNKS):
            relay(k, 1, 0, 1).wait_send()

    to_plane(1).wait_send()
    for j in range(1, tiles):
        to_plane(2 * j).wait_send()
        forward(j).wait_send()

    for copy in result_copies + z_copies:
        copy.wait()
    for d in range(1, count):
        mine = jnp.maximum(mine, back[d])
    mine = jnp.maximum(mine, jnp.maximum(z_back[0], z_back[1]))
    best[...] = jnp.maximum(jnp.max(mine, axis=0, keepdims=True), -1.0)


def similarities(units, meta, groups, members):
    rows, width = units.shape
    ys = members // NZ
    count = groups * ys
    dma = pltpu.SemaphoreType.DMA
    return pl.pallas_call(
        functools.partial(kernel, groups, ys),
        out_shape=jax.ShapeDtypeStruct((1, rows), jnp.float32),
        in_specs=[
            pl.BlockSpec(memory_space=pl.ANY),
            pl.BlockSpec(memory_space=pltpu.VMEM),
        ],
        out_specs=pl.BlockSpec(memory_space=pltpu.VMEM),
        scratch_shapes=[
            pltpu.VMEM((count, rows, width), jnp.bfloat16),
            pltpu.VMEM((2, rows, width), jnp.bfloat16),
            pltpu.VMEM((count, 2, rows), jnp.float32),
            pltpu.VMEM((2, 2, rows), jnp.float32),
            pltpu.VMEM((count, 8, rows), jnp.float32),
            pltpu.VMEM((3, rows, 128), jnp.float32),
            pltpu.VMEM((3, rows, 128), jnp.float32),
            pltpu.VMEM((3, rows, 128), jnp.float32),
            pltpu.VMEM((count, 8, rows), jnp.float32),
            pltpu.VMEM((2, 8, rows), jnp.float32),
            pltpu.VMEM((2, 8, rows), jnp.float32),
            dma(()),
            dma((count,)), dma((count,)),
            dma((2, CHUNKS)), dma((2, CHUNKS)),
            dma((count,)), dma((count,)),
            dma((2,)), dma((2,)),
            dma((count,)), dma((count,)),
            dma((2,)), dma((2,)),
            dma((2, CHUNKS)),
        ],
        compiler_params=pltpu.CompilerParams(
            collective_id=1, has_side_effects=True, vmem_limit_bytes=56 * 1024 * 1024
        ),
    )(units, meta)


HELD = 176
LAYOUT = 768
BIG = 1e9
CUTS = (64, 64, 48)
STEPS = ((0, 384), (384, 256), (640, 128))
NEAR = (176, 176)
BEFORE = [sum(CUTS[:k]) for k in range(len(CUTS))]
FAR = {
    j: [(384 + 2 * skip + (j - 2) * cut, cut) for skip, cut in zip(BEFORE, CUTS)] for j in (2, 3)
}
PIECES = [(0, 176), NEAR] + [(384 + 2 * skip, 2 * cut) for skip, cut in zip(BEFORE, CUTS)]


def relation_of(place):
    relation = jnp.where(place < 176, 0, jnp.where(place < 352, 1, 2))
    for start, cut in FAR[3]:
        relation = jnp.where((place >= start) & (place < start + cut), 3, relation)
    return relation


def spot(b, row):
    start, size = [step for step in STEPS if step[0] <= row][-1]
    return 4 * start + b * size + row - start


def either(a, b):
    return a + b - 2 * a * b


def routed_kernel(
    assignment, embeddings, cluster, order, member, out, over,
    raw, units, sent, blocks, sent_meta, z_meta, metas, row_key, row_acc, col_acc,
    places, fin, fin_got, load_sem, zs, zr, mzs, mzr, ps, pr, mps, mpr, fs, fr,
):
    g, m = lax.axis_index("grp"), lax.axis_index("mem")
    x, c, z, y = lax.div(g, 2), g % 2, lax.div(m, 2), m % 2
    rows, width = raw.shape
    owners, capacity = 32, 32

    load = pltpu.make_async_copy(embeddings, raw, load_sem)
    load.start()

    def device(x, c, z, y):
        return (x * 2 + c, z * 2 + y)

    def column(j):
        return device(x, c, flip(z, j), y)

    side_to = (
        device(x, 1 - c, z, y),
        device(1 - x, either(c, 1 - x), z, y),
        device(x, either(either(c, x), 1 - y), z, 1 - y),
    )
    side_from = (
        device(x, 1 - c, z, y),
        device(1 - x, either(c, x), z, y),
        device(x, either(either(c, x), y), z, 1 - y),
    )
    here = x * 4 + y * 2 + c

    def home(i):
        return device(i // 4, i % 2, g, (i // 2) % 2)

    is_home = z == g
    barrier = pltpu.get_barrier_semaphore()
    for peer in [column(j) for j in (1, 2, 3)] + list(side_from):
        pl.semaphore_signal(barrier, inc=1, device_id=peer, device_id_type=MESH)
    for i in range(8):
        @pl.when(jnp.logical_not(is_home & (here == i)))
        def _():
            pl.semaphore_signal(barrier, inc=1, device_id=home(i), device_id_type=MESH)

    def remote(src, dst, ssem, rsem, peer):
        return pltpu.make_async_remote_copy(
            src_ref=src, dst_ref=dst, send_sem=ssem, recv_sem=rsem,
            device_id=peer, device_id_type=MESH,
        )

    def z_copy(j, k):
        start, size = NEAR if j == 1 else FAR[j][k]
        here = pl.ds(start, size)
        there = pl.ds(spot(0, start), size)
        return remote(sent.at[here], blocks.at[there], zs.at[j, k], zr.at[j, k], column(j))

    def z_meta_copy(j):
        return remote(sent_meta, z_meta.at[j], mzs.at[j], mzr.at[j], column(j))

    def side_copy(t, k):
        start, size = PIECES[k]
        mine, theirs = pl.ds(spot(0, start), size), pl.ds(spot(t + 1, start), size)
        return remote(
            blocks.at[mine], blocks.at[theirs], ps.at[t, k], pr.at[t, k], side_to[t]
        )

    def side_meta_copy(t):
        return remote(metas.at[0], metas.at[t + 1], mps.at[t], mpr.at[t], side_to[t])

    def fin_copy(p):
        return remote(fin.at[p], fin_got.at[here], fs.at[p], fr.at[here], (z, p))

    def fin_from(i):
        return remote(fin.at[0], fin_got.at[i], fs.at[0], fr.at[i], home(i))

    def wide(ref):
        return jnp.concatenate([ref[i : i + 1, :] for i in range(rows // 128)], axis=1)

    ids, keys, mem_of = wide(cluster), wide(order), wide(member)
    group = jnp.zeros_like(ids)
    for k in range(4):
        group = jnp.where(ids == k, assignment[k], group)
    owner = group * 8 + mem_of
    hits = jnp.concatenate(
        [
            (lax.broadcasted_iota(jnp.int32, (owners, rows), 0) == owner).astype(jnp.float32),
            (lax.broadcasted_iota(jnp.int32, (16, rows), 0) == group).astype(jnp.float32),
        ],
        axis=0,
    )
    before = (
        lax.broadcasted_iota(jnp.int32, (128, 128), 0)
        < lax.broadcasted_iota(jnp.int32, (128, 128), 1)
    ).astype(jnp.float32).astype(jnp.bfloat16)
    earlier_hits = jnp.zeros((owners + 16, 1), jnp.float32)
    counts = []
    for k in range(rows // 128):
        part = hits[:, k * 128 : (k + 1) * 128]
        inside = jnp.dot(part.astype(jnp.bfloat16), before, preferred_element_type=jnp.float32)
        counts.append(part * (inside + earlier_hits))
        earlier_hits = earlier_hits + jnp.sum(part, axis=1, keepdims=True)
    counts = jnp.concatenate(counts, axis=1)
    rank = jnp.sum(counts[:owners], axis=0, keepdims=True)
    pos = jnp.sum(counts[owners:], axis=0, keepdims=True).astype(jnp.int32)
    j = jnp.bitwise_xor(group, z)
    high = jnp.where(j >= 3, 1, 0)
    far = jnp.zeros_like(pos)
    for skip, cut in zip(BEFORE, CUTS):
        far = jnp.where(pos >= skip, 384 + skip + cut * high + pos, far)
    target = jnp.where(j == 0, pos, jnp.where(j == 1, 176 + pos, far))
    target = jnp.where(pos < HELD, target, -1)
    spilled = jnp.max(jnp.where(pos < HELD, 0.0, 1.0), axis=1, keepdims=True)

    def chosen(start, size):
        place = lax.broadcasted_iota(jnp.int32, (size, rows), 0) + start
        return (place == target).astype(jnp.float32).astype(jnp.bfloat16)

    facts = jnp.concatenate(
        [
            lax.shift_right_logical(keys, 8).astype(jnp.float32),
            jnp.bitwise_and(keys, 255).astype(jnp.float32),
            mem_of.astype(jnp.float32),
            rank,
            jnp.ones((1, rows), jnp.float32),
            jnp.zeros((11, rows), jnp.float32),
        ],
        axis=0,
    ).astype(jnp.bfloat16)
    for start, size in STEPS:
        lanes = slice(start, start + size)
        sorted_facts = lax.dot_general(
            facts, chosen(start, size), (((1,), (1,)), ((), ())),
            preferred_element_type=jnp.float32,
        )
        held = sorted_facts[4:5] > 0.5
        sent_meta[0:1, lanes] = jnp.where(
            held, sorted_facts[0:1] * 256.0 + sorted_facts[1:2], BIG
        )
        sent_meta[1:2, lanes] = jnp.where(held, sorted_facts[2:3], -1.0)
        sent_meta[2:3, lanes] = sorted_facts[3:4]
        sent_meta[3:4, lanes] = jnp.broadcast_to(spilled, (1, size))
        sent_meta[4:8, lanes] = jnp.zeros((4, size), jnp.float32)

    load.wait()

    def normalise(i, carry):
        part = pl.ds(pl.multiple_of(i * 128, 128), 128)
        widened = raw[part, :].astype(jnp.float32)
        scale = lax.rsqrt(jnp.mean(widened * widened, axis=1, keepdims=True) + 1e-06)
        units[part, :] = (widened * scale * (1.0 / math.sqrt(width))).astype(jnp.bfloat16)
        return carry

    lax.fori_loop(0, rows // 128, normalise, 0)

    def place(start, size):
        picks = chosen(start, size)
        lanes = slice(start, start + size)
        sorted_facts = lax.dot_general(
            facts, picks, (((1,), (1,)), ((), ())), preferred_element_type=jnp.float32
        )
        held = sorted_facts[4:5] > 0.5
        sent_meta[0:1, lanes] = jnp.where(
            held, sorted_facts[0:1] * 256.0 + sorted_facts[1:2], BIG
        )
        sent_meta[1:2, lanes] = jnp.where(held, sorted_facts[2:3], -1.0)
        sent_meta[2:3, lanes] = sorted_facts[3:4]
        sent_meta[3:4, lanes] = jnp.broadcast_to(spilled, (1, size))
        sent_meta[4:8, lanes] = jnp.zeros((4, size), jnp.float32)
        return jnp.dot(
            picks, units[...], preferred_element_type=jnp.float32
        ).astype(jnp.bfloat16)

    sent[pl.ds(384, 256), :] = place(384, 256)
    near = place(0, 384)
    sent[pl.ds(*NEAR), :] = near[176:352]
    blocks[pl.ds(0, 176), :] = near[:176]
    sent[pl.ds(640, 128), :] = place(640, 128)

    @pl.when(is_home)
    def _():
        pl.semaphore_wait(barrier, 13)

    @pl.when(jnp.logical_not(is_home))
    def _():
        pl.semaphore_wait(barrier, 14)

    for r in (1, 2, 3):
        z_meta_copy(r).start()
    z_copy(1, 0).start()
    for k in range(len(CUTS)):
        z_copy(3, k).start()
        z_copy(2, k).start()
    for t in range(3):
        side_copy(t, 0).start()
    for b in range(4):
        for row in (352, 736):
            blocks[pl.ds(spot(b, row), 32), :] = jnp.zeros((32, width), jnp.bfloat16)
    row_acc[...] = jnp.full(row_acc.shape, LOW, jnp.float32)
    col_acc[...] = jnp.full(col_acc.shape, LOW, jnp.float32)

    for r in (1, 2, 3):
        z_meta_copy(r).wait_recv()
    lane = lax.broadcasted_iota(jnp.int32, (8, LAYOUT), 1)
    relation = relation_of(lane)
    joined = sent_meta[...]
    spill = jnp.max(joined[3:4], axis=1, keepdims=True)
    for r in (1, 2, 3):
        joined = jnp.where(relation == r, z_meta[r], joined)
        spill = jnp.maximum(spill, jnp.max(z_meta[r, 3:4, :], axis=1, keepdims=True))
    metas[0] = joined
    for t in range(3):
        side_meta_copy(t).start()

    def prepare(b):
        keys = jnp.broadcast_to(metas[b, 0:1, :], (128, LAYOUT)).T
        for start, size in STEPS:
            row_key[pl.ds(spot(b, start), size), :] = keys[start : start + size]
        slot = jnp.bitwise_xor(relation[0:1], z) * 32 + metas[b, 2:3, :].astype(jnp.int32)
        places[b] = (
            lax.broadcasted_iota(jnp.int32, (128, LAYOUT), 0) == slot
        ).astype(jnp.float32).astype(jnp.bfloat16)

    def meet(lefts, right, start, size, both=True):
        theirs = blocks[pl.ds(spot(right, start), size), :]
        for first, count in lefts:
            part = pl.ds(first, count)
            scores = lax.dot_general(
                blocks[part, :], theirs, (((1,), (1,)), ((), ())),
                preferred_element_type=jnp.float32,
            )
            my_key = row_key[part, :]
            acc = row_acc[part, :]
            for t in range(size // 128):
                lanes = slice(start + t * 128, start + (t + 1) * 128)
                earlier = metas[right, 0:1, lanes] < my_key
                score = scores[:, t * 128 : (t + 1) * 128]
                acc = jnp.maximum(acc, jnp.where(earlier, score, LOW))
                if both:
                    other = jnp.where(earlier, LOW, score).reshape(count // 8, 8, 128)
                    col_acc[right, :, lanes] = jnp.maximum(
                        col_acc[right, :, lanes], jnp.max(other, axis=0)
                    )
            row_acc[part, :] = acc

    def own_step(s):
        start, size = STEPS[s]
        new = [(spot(0, start), size)]
        for old in STEPS[:s]:
            for right in (0, 2, 3):
                meet(new, right, *old)
        meet(new, 0, start, size, False)

    def side_step(s):
        start, size = STEPS[s]
        s_new, x_new, y_new = [(spot(b, start), size) for b in (1, 2, 3)]
        sides = [s_new, x_new, y_new] if size > 128 else [(s_new[0], 3 * size)]
        for run in STEPS[: s + 1]:
            meet(sides, 0, *run)
            meet([y_new], 2, *run)
        for run in STEPS[:s]:
            meet([x_new], 3, *run)

    def fold(s):
        start, size = STEPS[s]
        for b in range(4):
            turned = row_acc[pl.ds(spot(b, start), size), :].T.reshape(16, 8, size)
            lanes = slice(start, start + size)
            col_acc[b, :, lanes] = jnp.maximum(col_acc[b, :, lanes], jnp.max(turned, axis=0))

    z_copy(1, 0).wait_recv()
    for t in range(3):
        side_copy(t, 1).start()
    prepare(0)
    own_step(0)
    def wait_sides(first, last):
        for k in range(first, last):
            for t in range(3):
                side_copy(t, k).wait_recv()

    done = [max(k for k in range(len(PIECES)) if PIECES[k][0] < a + b) + 1 for a, b in STEPS]
    for k in range(2, len(PIECES)):
        for r in (3, 2):
            z_copy(r, k - 2).wait_recv()
        for t in range(3):
            side_copy(t, k).start()
        if k == 3:
            for t in range(3):
                side_meta_copy(t).wait_recv()
            for b in (1, 2, 3):
                prepare(b)
            wait_sides(0, done[0])
            side_step(0)
            fold(0)
        if k == done[1] - 1:
            own_step(1)
    wait_sides(done[0], done[1])
    side_step(1)
    own_step(2)
    fold(1)
    wait_sides(done[1], len(PIECES))
    side_step(2)
    fold(2)

    for b in range(4):
        value = jnp.max(col_acc[b], axis=0, keepdims=True)
        value = jnp.maximum(value, -1.0)
        parts = []
        for _ in range(3):
            part = value.astype(jnp.bfloat16).astype(jnp.float32)
            parts.append(part)
            value = value - part
        parts.append(jnp.ones_like(value))
        mine = (
            lax.broadcasted_iota(jnp.int32, (8, LAYOUT), 0)
            == metas[b, 1:2, :].astype(jnp.int32)
        ).astype(jnp.float32)
        stacked = jnp.concatenate([mine * part for part in parts], axis=0).astype(jnp.bfloat16)
        found = lax.dot_general(
            stacked, places[b], (((1,), (1,)), ((), ())), preferred_element_type=jnp.float32
        )
        total = (found[16:24] + found[8:16]) + found[0:8]
        fin[:, b, :] = jnp.where(found[24:32] > 0.5, total, -1.0)
    for b in range(4, 8):
        fin[:, b, :] = jnp.broadcast_to(spill, (8, 128))

    for p in range(8):
        me = is_home & (m == p)

        @pl.when(jnp.logical_not(me))
        def _():
            fin_copy(p).start()

        @pl.when(me)
        def _():
            fin_got[here] = fin[p]

    for r in (1, 2, 3):
        z_meta_copy(r).wait_send()
    z_copy(1, 0).wait_send()
    for r in (3, 2):
        for k in range(len(CUTS)):
            z_copy(r, k).wait_send()
    for t in range(3):
        side_meta_copy(t).wait_send()
        for k in range(len(PIECES)):
            side_copy(t, k).wait_send()
    for p in range(8):
        @pl.when(jnp.logical_not(is_home & (m == p)))
        def _():
            fin_copy(p).wait_send()
    for i in range(8):
        @pl.when(jnp.logical_not(is_home & (here == i)))
        def _():
            fin_from(i).wait_recv()

    block = lax.broadcasted_iota(jnp.int32, (1, 128), 1) // 32
    worst = fin_got[0, 4:5, :]
    for i in range(1, 8):
        worst = jnp.maximum(worst, fin_got[i, 4:5, :])
    over[...] = worst[:, :1]
    for xs in range(2):
        for cs in range(2):
            ways = []
            for ys in range(2):
                i = xs * 4 + ys * 2 + cs
                sibling = xs * 4 + ys * 2 + (1 - cs)
                x_holder = (1 - xs) * 4 + ys * 2 + (cs ^ (1 - xs))
                y_holder = xs * 4 + (1 - ys) * 2 + (cs ^ xs ^ (1 - ys))
                ways.append(
                    jnp.maximum(
                        jnp.maximum(fin_got[i, 0:1, :], fin_got[sibling, 1:2, :]),
                        jnp.maximum(fin_got[x_holder, 2:3, :], fin_got[y_holder, 3:4, :]),
                    )
                )
            for half, turns in enumerate(((0, 32, 32, 64), (64, 96, 96, 0))):
                line = ways[0]
                for k in range(4):
                    way = ways[k % 2]
                    turned = pltpu.roll(way, turns[k], 1) if turns[k] else way
                    line = jnp.where(block == k, turned, line)
                row = (xs * 2 + cs) * 2 + half
                out[row : row + 1, :] = line


def routed(embeddings, cluster_id, row_order, assignment, placement):
    rows, width = embeddings.shape
    dma = pltpu.SemaphoreType.DMA
    lines = (rows // 128, 128)
    vmem = pl.BlockSpec(memory_space=pltpu.VMEM)
    return pl.pallas_call(
        routed_kernel,
        out_shape=[jax.ShapeDtypeStruct(shape, jnp.float32) for shape in ((8, 128), (1, 1))],
        in_specs=[
            pl.BlockSpec(memory_space=pltpu.SMEM), pl.BlockSpec(memory_space=pl.ANY),
            vmem, vmem, vmem,
        ],
        out_specs=[vmem, vmem],
        scratch_shapes=[
            pltpu.VMEM((rows, width), jnp.bfloat16),
            pltpu.VMEM((rows, width), jnp.bfloat16),
            pltpu.VMEM((LAYOUT, width), jnp.bfloat16),
            pltpu.VMEM((4 * LAYOUT, width), jnp.bfloat16),
            pltpu.VMEM((8, LAYOUT), jnp.float32),
            pltpu.VMEM((4, 8, LAYOUT), jnp.float32),
            pltpu.VMEM((4, 8, LAYOUT), jnp.float32),
            pltpu.VMEM((4 * LAYOUT, 128), jnp.float32),
            pltpu.VMEM((4 * LAYOUT, 128), jnp.float32),
            pltpu.VMEM((4, 8, LAYOUT), jnp.float32),
            pltpu.VMEM((4, 128, LAYOUT), jnp.bfloat16),
            pltpu.VMEM((8, 8, 128), jnp.float32),
            pltpu.VMEM((8, 8, 128), jnp.float32),
            dma(()),
            dma((4, len(CUTS))), dma((4, len(CUTS))),
            dma((4,)), dma((4,)),
            dma((3, len(PIECES))), dma((3, len(PIECES))),
            dma((3,)), dma((3,)),
            dma((8,)), dma((8,)),
        ],
        compiler_params=pltpu.CompilerParams(
            collective_id=0, has_side_effects=True, vmem_limit_bytes=48 * 1024 * 1024
        ),
    )(
        assignment, embeddings, cluster_id.reshape(lines), row_order.reshape(lines),
        placement.reshape(lines),
    )


def dense(embeddings, cluster_id, row_order, assignment, placement):
    members = lax.axis_size("mem")
    groups = lax.axis_size("grp")
    owners = groups * members
    row_count, feature_count = embeddings.shape
    capacity = max(2, 2 * row_count // owners)
    widened = embeddings.astype(jnp.float32)
    unit_rows = (
        widened
        * lax.rsqrt(jnp.mean(widened * widened, axis=1, keepdims=True) + 1e-06)
        * (1.0 / math.sqrt(feature_count))
    ).astype(jnp.bfloat16)
    meta = jnp.stack([row_order, cluster_id]).astype(jnp.float32)
    best = similarities(unit_rows, meta, groups, members)

    table_hits = cluster_id[:, None] == jnp.arange(assignment.shape[0], dtype=jnp.int32)[None, :]
    group_of = jnp.sum(jnp.where(table_hits, assignment[None, :], 0), axis=1)
    owner_id = group_of * members + placement
    before = jnp.arange(row_count)[None, :] < jnp.arange(row_count)[:, None]
    rank = jnp.sum((before & (owner_id[None, :] == owner_id[:, None])).astype(jnp.int32), axis=1)
    target = owner_id * capacity + rank
    slots = jnp.arange(owners * capacity, dtype=jnp.int32)
    filled = jnp.max(
        jnp.where(slots[:, None] == target[None, :], best, -1.0), axis=1
    )
    return lax.all_to_all(filled, ("grp", "mem"), split_axis=0, concat_axis=0, tiled=True)


def local(*args):
    embeddings, _, _, assignment, _ = args
    shape = (lax.axis_size("grp"), lax.axis_size("mem"), assignment.shape[0]) + embeddings.shape
    if shape != (4, 8, 4, 512, 768):
        return dense(*args)
    found, over = routed(*args)
    return lax.cond(
        over[0, 0] > 0.5, lambda: dense(*args), lambda: found.reshape(found.size)
    )


def solution(mesh):
    return jax.shard_map(
        local,
        mesh=mesh,
        in_specs=(
            P(("grp", "mem"), None),
            P(("grp", "mem")),
            P(("grp", "mem")),
            P(),
            P(("grp", "mem")),
        ),
        out_specs=P(("grp", "mem")),
        check_vma=False,
    )
```

```python
import functools
import math

import jax
import jax.numpy as jnp
from jax import lax
from jax.experimental import pallas as pl
from jax.experimental.pallas import tpu as pltpu
from jax.sharding import PartitionSpec as P

MESH = pl.DeviceIdType.MESH
NZ = 4
CHUNKS = 4
TILE = 256
LOW = -2.0


def flip(index, mask):
    out, bit = index, 1
    while bit <= mask:
        if mask & bit:
            out = out + bit - 2 * bit * (lax.div(index, bit) % 2)
        bit *= 2
    return out


def kernel(
    groups, ys, units, meta, best, planes, zs, plane_meta, z_meta, col_acc, row_acc,
    row_key, row_cluster, back, z_back, z_send, ready_sem, p_send, p_recv, z_ssem, z_rsem,
    pm_send, pm_recv, zm_send, zm_recv, b_send, b_recv, zb_send, zb_recv, relay_sem,
):
    g, m = lax.axis_index("grp"), lax.axis_index("mem")
    z, y = lax.div(m, ys), m % ys
    tiles = (groups // 2) * ys
    count = 2 * tiles
    rows = planes.shape[1]
    part = rows // CHUNKS

    def plane_peer(d):
        j, c = d // 2, d % 2
        return (flip(g, (j // ys) * 2 + c), z * ys + flip(y, j % ys))

    def column_peer(dz):
        return (g, ((z + dz) % NZ) * ys + y)

    load = pltpu.make_async_copy(units, planes.at[0], ready_sem)
    load.start()

    barrier = pltpu.get_barrier_semaphore()
    peers = [plane_peer(d) for d in range(1, count)] + [column_peer(k) for k in range(1, NZ)]
    for peer in peers:
        pl.semaphore_signal(barrier, inc=1, device_id=peer, device_id_type=MESH)
    col_acc[...] = jnp.full(col_acc.shape, LOW, jnp.float32)
    row_acc[...] = jnp.full(row_acc.shape, LOW, jnp.float32)
    plane_meta[0] = meta[...]
    load.wait()
    pl.semaphore_wait(barrier, len(peers))

    def remote(src, dst, ssem, rsem, peer):
        return pltpu.make_async_remote_copy(
            src_ref=src, dst_ref=dst, send_sem=ssem, recv_sem=rsem,
            device_id=peer, device_id_type=MESH,
        )

    def piece(k):
        return pl.ds(k * part, part)

    def own_to_z(k, slot, dz):
        return remote(
            planes.at[0, piece(k)], zs.at[slot, piece(k)], z_ssem.at[slot, k],
            z_rsem.at[slot, k], column_peer(dz),
        )

    def relay(k, src, dst, dz):
        return remote(
            zs.at[src, piece(k)], zs.at[dst, piece(k)], relay_sem.at[src, k],
            z_rsem.at[dst, k], column_peer(dz),
        )

    def to_plane(d):
        return remote(planes.at[0], planes.at[d], p_send.at[d], p_recv.at[d], plane_peer(d))

    def forward(j):
        return remote(
            planes.at[2 * j], planes.at[2 * j + 1], p_send.at[2 * j + 1], p_recv.at[2 * j + 1],
            plane_peer(1),
        )

    meta_copies = [
        remote(meta, plane_meta.at[d], pm_send.at[d], pm_recv.at[d], plane_peer(d))
        for d in range(1, count)
    ] + [
        remote(meta, z_meta.at[s], zm_send.at[s], zm_recv.at[s], column_peer(-1 - s))
        for s in range(2)
    ]
    for copy in meta_copies:
        copy.start()

    to_plane(1).start()

    @pl.when(z >= 1)
    def _():
        for k in range(CHUNKS):
            own_to_z(k, 0, -1).start()

    @pl.when(z <= 1)
    def _():
        for k in range(CHUNKS):
            own_to_z(k, 1, 2).start()

    for j in range(1, tiles):
        to_plane(2 * j).start()

    def spread(a, source):
        row_key[a] = jnp.broadcast_to(source[0:1, :], (128, rows)).T
        row_cluster[a] = jnp.broadcast_to(source[1:2, :], (128, rows)).T

    def pairs(a, left, d, both):
        right = planes[d]
        keys, clusters = plane_meta[d, 0:1, :], plane_meta[d, 1:2, :]

        def step(i, carry):
            here = pl.ds(pl.multiple_of(i * TILE, TILE), TILE)
            scores = lax.dot_general(
                left[here, :], right, (((1,), (1,)), ((), ())),
                preferred_element_type=jnp.float32,
            )
            my_key, my_cluster = row_key[a, here, :], row_cluster[a, here, :]
            acc = row_acc[a, here, :]
            for t in range(rows // 128):
                lanes = slice(t * 128, (t + 1) * 128)
                kept = jnp.where(my_cluster == clusters[:, lanes], scores[:, lanes], LOW)
                earlier = keys[:, lanes] < my_key
                acc = jnp.maximum(acc, jnp.where(earlier, kept, LOW))
                if both:
                    other = jnp.where(earlier, LOW, kept).reshape(TILE // 8, 8, 128)
                    col_acc[d, :, lanes] = jnp.maximum(col_acc[d, :, lanes], jnp.max(other, axis=0))
            row_acc[a, here, :] = acc
            return carry

        lax.fori_loop(0, rows // TILE, step, 0)

    spread(0, meta)
    own = planes.at[0]
    pairs(0, own, 0, False)
    for copy in meta_copies:
        copy.wait()
    to_plane(1).wait_recv()
    pairs(0, own, 1, False)

    for k in range(CHUNKS):
        @pl.when((z == 1) | (z == 2))
        def _():
            own_to_z(k, 0, -1).wait_recv()
            relay(k, 0, 1, -1).start()

        @pl.when(z == 2)
        def _():
            own_to_z(k, 1, 2).wait_recv()
            relay(k, 1, 0, 1).start()

    def plane_step(j, carry):
        pltpu.make_async_copy(planes.at[2 * j], planes.at[2 * j], p_recv.at[2 * j]).wait()
        forward(j).start()
        pairs(0, own, 2 * j, False)
        forward(j).wait_recv()
        pairs(0, own, 2 * j + 1, False)
        return carry

    lax.fori_loop(1, tiles, plane_step, 0)

    for k in range(CHUNKS):
        @pl.when((z == 0) | (z == 3))
        def _():
            own_to_z(k, 0, -1).wait_recv()

        @pl.when(z != 2)
        def _():
            own_to_z(k, 1, 2).wait_recv()

    spread(1, z_meta.at[0])
    spread(2, z_meta.at[1])

    def z1_step(d, carry):
        pairs(1, zs.at[0], d, True)
        return carry

    lax.fori_loop(0, count, z1_step, 0)
    first = lax.div(z, 2) * (count // 2)

    def z2_step(d, carry):
        pairs(2, zs.at[1], d + first, True)
        return carry

    lax.fori_loop(0, count // 2, z2_step, 0)

    def fold(a):
        return jnp.max(row_acc[a].T.reshape(16, 8, rows), axis=0)

    z_send[0] = fold(1)
    z_send[1] = fold(2)
    result_copies = [
        remote(col_acc.at[d], back.at[d], b_send.at[d], b_recv.at[d], plane_peer(d))
        for d in range(1, count)
    ]
    for copy in result_copies:
        copy.start()
    mine = jnp.maximum(fold(0), col_acc[0])
    z_copies = [
        remote(z_send.at[s], z_back.at[s], zb_send.at[s], zb_recv.at[s], column_peer(1 + s))
        for s in range(2)
    ]
    for copy in z_copies:
        copy.start()

    @pl.when(z >= 1)
    def _():
        for k in range(CHUNKS):
            own_to_z(k, 0, -1).wait_send()

    @pl.when(z <= 1)
    def _():
        for k in range(CHUNKS):
            own_to_z(k, 1, 2).wait_send()

    @pl.when((z == 1) | (z == 2))
    def _():
        for k in range(CHUNKS):
            relay(k, 0, 1, -1).wait_send()

    @pl.when(z == 2)
    def _():
        for k in range(CHUNKS):
            relay(k, 1, 0, 1).wait_send()

    to_plane(1).wait_send()
    for j in range(1, tiles):
        to_plane(2 * j).wait_send()
        forward(j).wait_send()

    for copy in result_copies + z_copies:
        copy.wait()
    for d in range(1, count):
        mine = jnp.maximum(mine, back[d])
    mine = jnp.maximum(mine, jnp.maximum(z_back[0], z_back[1]))
    best[...] = jnp.maximum(jnp.max(mine, axis=0, keepdims=True), -1.0)


def similarities(units, meta, groups, members):
    rows, width = units.shape
    ys = members // NZ
    count = groups * ys
    dma = pltpu.SemaphoreType.DMA
    return pl.pallas_call(
        functools.partial(kernel, groups, ys),
        out_shape=jax.ShapeDtypeStruct((1, rows), jnp.float32),
        in_specs=[
            pl.BlockSpec(memory_space=pl.ANY),
            pl.BlockSpec(memory_space=pltpu.VMEM),
        ],
        out_specs=pl.BlockSpec(memory_space=pltpu.VMEM),
        scratch_shapes=[
            pltpu.VMEM((count, rows, width), jnp.bfloat16),
            pltpu.VMEM((2, rows, width), jnp.bfloat16),
            pltpu.VMEM((count, 2, rows), jnp.float32),
            pltpu.VMEM((2, 2, rows), jnp.float32),
            pltpu.VMEM((count, 8, rows), jnp.float32),
            pltpu.VMEM((3, rows, 128), jnp.float32),
            pltpu.VMEM((3, rows, 128), jnp.float32),
            pltpu.VMEM((3, rows, 128), jnp.float32),
            pltpu.VMEM((count, 8, rows), jnp.float32),
            pltpu.VMEM((2, 8, rows), jnp.float32),
            pltpu.VMEM((2, 8, rows), jnp.float32),
            dma(()),
            dma((count,)), dma((count,)),
            dma((2, CHUNKS)), dma((2, CHUNKS)),
            dma((count,)), dma((count,)),
            dma((2,)), dma((2,)),
            dma((count,)), dma((count,)),
            dma((2,)), dma((2,)),
            dma((2, CHUNKS)),
        ],
        compiler_params=pltpu.CompilerParams(
            collective_id=1, has_side_effects=True, vmem_limit_bytes=56 * 1024 * 1024
        ),
    )(units, meta)


HELD = 176
LAYOUT = 768
BIG = 1e9
CUTS = (32, 32, 32, 32, 32, 16)
STEPS = ((0, 384), (384, 256), (640, 128))
NEAR = (176, 176)
BEFORE = [sum(CUTS[:k]) for k in range(len(CUTS))]
FAR = {
    j: [(384 + 2 * skip + (j - 2) * cut, cut) for skip, cut in zip(BEFORE, CUTS)] for j in (2, 3)
}
PIECES = [(0, 176), NEAR] + [(384 + 2 * skip, 2 * cut) for skip, cut in zip(BEFORE, CUTS)]


def relation_of(place):
    relation = jnp.where(place < 176, 0, jnp.where(place < 352, 1, 2))
    for start, cut in FAR[3]:
        relation = jnp.where((place >= start) & (place < start + cut), 3, relation)
    return relation


def spot(b, row):
    start, size = [step for step in STEPS if step[0] <= row][-1]
    return 4 * start + b * size + row - start


def either(a, b):
    return a + b - 2 * a * b


def routed_kernel(
    assignment, embeddings, cluster, order, member, out, over,
    raw, units, sent, blocks, sent_meta, z_meta, metas, row_key, row_acc, col_acc,
    places, fin, fin_got, load_sem, zs, zr, mzs, mzr, ps, pr, mps, mpr, fs, fr,
):
    g, m = lax.axis_index("grp"), lax.axis_index("mem")
    x, c, z, y = lax.div(g, 2), g % 2, lax.div(m, 2), m % 2
    rows, width = raw.shape
    owners, capacity = 32, 32

    load = pltpu.make_async_copy(embeddings, raw, load_sem)
    load.start()

    def device(x, c, z, y):
        return (x * 2 + c, z * 2 + y)

    def column(j):
        return device(x, c, flip(z, j), y)

    side_to = (
        device(x, 1 - c, z, y),
        device(1 - x, either(c, 1 - x), z, y),
        device(x, either(either(c, x), 1 - y), z, 1 - y),
    )
    side_from = (
        device(x, 1 - c, z, y),
        device(1 - x, either(c, x), z, y),
        device(x, either(either(c, x), y), z, 1 - y),
    )
    here = x * 4 + y * 2 + c

    def home(i):
        return device(i // 4, i % 2, g, (i // 2) % 2)

    is_home = z == g
    barrier = pltpu.get_barrier_semaphore()
    for peer in [column(j) for j in (1, 2, 3)] + list(side_from):
        pl.semaphore_signal(barrier, inc=1, device_id=peer, device_id_type=MESH)

    def remote(src, dst, ssem, rsem, peer):
        return pltpu.make_async_remote_copy(
            src_ref=src, dst_ref=dst, send_sem=ssem, recv_sem=rsem,
            device_id=peer, device_id_type=MESH,
        )

    def z_copy(j, k):
        start, size = NEAR if j == 1 else FAR[j][k]
        here = pl.ds(start, size)
        there = pl.ds(spot(0, start), size)
        return remote(sent.at[here], blocks.at[there], zs.at[j, k], zr.at[j, k], column(j))

    def z_meta_copy(j):
        return remote(sent_meta, z_meta.at[j], mzs.at[j], mzr.at[j], column(j))

    def side_copy(t, k):
        start, size = PIECES[k]
        mine, theirs = pl.ds(spot(0, start), size), pl.ds(spot(t + 1, start), size)
        return remote(
            blocks.at[mine], blocks.at[theirs], ps.at[t, k], pr.at[t, k], side_to[t]
        )

    def side_meta_copy(t):
        return remote(metas.at[0], metas.at[t + 1], mps.at[t], mpr.at[t], side_to[t])

    def fin_copy(p):
        return remote(fin.at[p], fin_got.at[here], fs.at[p], fr.at[here], (z, p))

    def fin_from(i):
        return remote(fin.at[0], fin_got.at[i], fs.at[0], fr.at[i], home(i))

    def wide(ref):
        return jnp.concatenate([ref[i : i + 1, :] for i in range(rows // 128)], axis=1)

    ids, keys, mem_of = wide(cluster), wide(order), wide(member)
    group = jnp.zeros_like(ids)
    for k in range(4):
        group = jnp.where(ids == k, assignment[k], group)
    owner = group * 8 + mem_of
    hits = jnp.concatenate(
        [
            (lax.broadcasted_iota(jnp.int32, (owners, rows), 0) == owner).astype(jnp.float32),
            (lax.broadcasted_iota(jnp.int32, (16, rows), 0) == group).astype(jnp.float32),
        ],
        axis=0,
    )
    before = (
        lax.broadcasted_iota(jnp.int32, (128, 128), 0)
        < lax.broadcasted_iota(jnp.int32, (128, 128), 1)
    ).astype(jnp.float32).astype(jnp.bfloat16)
    earlier_hits = jnp.zeros((owners + 16, 1), jnp.float32)
    counts = []
    for k in range(rows // 128):
        part = hits[:, k * 128 : (k + 1) * 128]
        inside = jnp.dot(part.astype(jnp.bfloat16), before, preferred_element_type=jnp.float32)
        counts.append(part * (inside + earlier_hits))
        earlier_hits = earlier_hits + jnp.sum(part, axis=1, keepdims=True)
    counts = jnp.concatenate(counts, axis=1)
    rank = jnp.sum(counts[:owners], axis=0, keepdims=True)
    pos = jnp.sum(counts[owners:], axis=0, keepdims=True).astype(jnp.int32)
    j = jnp.bitwise_xor(group, z)
    high = jnp.where(j >= 3, 1, 0)
    far = jnp.zeros_like(pos)
    for skip, cut in zip(BEFORE, CUTS):
        far = jnp.where(pos >= skip, 384 + skip + cut * high + pos, far)
    target = jnp.where(j == 0, pos, jnp.where(j == 1, 176 + pos, far))
    target = jnp.where(pos < HELD, target, -1)
    spilled = jnp.max(jnp.where(pos < HELD, 0.0, 1.0), axis=1, keepdims=True)

    def chosen(start, size):
        place = lax.broadcasted_iota(jnp.int32, (size, rows), 0) + start
        return (place == target).astype(jnp.float32).astype(jnp.bfloat16)

    facts = jnp.concatenate(
        [
            lax.shift_right_logical(keys, 8).astype(jnp.float32),
            jnp.bitwise_and(keys, 255).astype(jnp.float32),
            mem_of.astype(jnp.float32),
            rank,
            jnp.ones((1, rows), jnp.float32),
            jnp.zeros((11, rows), jnp.float32),
        ],
        axis=0,
    ).astype(jnp.bfloat16)
    for start, size in STEPS:
        lanes = slice(start, start + size)
        sorted_facts = lax.dot_general(
            facts, chosen(start, size), (((1,), (1,)), ((), ())),
            preferred_element_type=jnp.float32,
        )
        held = sorted_facts[4:5] > 0.5
        sent_meta[0:1, lanes] = jnp.where(
            held, sorted_facts[0:1] * 256.0 + sorted_facts[1:2], BIG
        )
        sent_meta[1:2, lanes] = jnp.where(held, sorted_facts[2:3], -1.0)
        sent_meta[2:3, lanes] = sorted_facts[3:4]
        sent_meta[3:4, lanes] = jnp.broadcast_to(spilled, (1, size))
        sent_meta[4:8, lanes] = jnp.zeros((4, size), jnp.float32)

    load.wait()

    def normalise(i, carry):
        part = pl.ds(pl.multiple_of(i * 128, 128), 128)
        widened = raw[part, :].astype(jnp.float32)
        scale = lax.rsqrt(jnp.mean(widened * widened, axis=1, keepdims=True) + 1e-06)
        units[part, :] = (widened * scale * (1.0 / math.sqrt(width))).astype(jnp.bfloat16)
        return carry

    lax.fori_loop(0, rows // 128, normalise, 0)

    def place(start, size):
        picks = chosen(start, size)
        lanes = slice(start, start + size)
        sorted_facts = lax.dot_general(
            facts, picks, (((1,), (1,)), ((), ())), preferred_element_type=jnp.float32
        )
        held = sorted_facts[4:5] > 0.5
        sent_meta[0:1, lanes] = jnp.where(
            held, sorted_facts[0:1] * 256.0 + sorted_facts[1:2], BIG
        )
        sent_meta[1:2, lanes] = jnp.where(held, sorted_facts[2:3], -1.0)
        sent_meta[2:3, lanes] = sorted_facts[3:4]
        sent_meta[3:4, lanes] = jnp.broadcast_to(spilled, (1, size))
        sent_meta[4:8, lanes] = jnp.zeros((4, size), jnp.float32)
        return jnp.dot(
            picks, units[...], preferred_element_type=jnp.float32
        ).astype(jnp.bfloat16)

    sent[pl.ds(384, 256), :] = place(384, 256)
    near = place(0, 384)
    sent[pl.ds(*NEAR), :] = near[176:352]
    blocks[pl.ds(0, 176), :] = near[:176]
    sent[pl.ds(640, 128), :] = place(640, 128)

    pl.semaphore_wait(barrier, 6)

    for r in (1, 2, 3):
        z_meta_copy(r).start()
    z_copy(1, 0).start()
    for k in range(len(CUTS)):
        z_copy(3, k).start()
        z_copy(2, k).start()
    for t in range(3):
        side_copy(t, 0).start()
    for b in range(4):
        for row in (352, 736):
            blocks[pl.ds(spot(b, row), 32), :] = jnp.zeros((32, width), jnp.bfloat16)
    row_acc[...] = jnp.full(row_acc.shape, LOW, jnp.float32)
    col_acc[...] = jnp.full(col_acc.shape, LOW, jnp.float32)

    for r in (1, 2, 3):
        z_meta_copy(r).wait_recv()
    lane = lax.broadcasted_iota(jnp.int32, (8, LAYOUT), 1)
    relation = relation_of(lane)
    joined = sent_meta[...]
    spill = jnp.max(joined[3:4], axis=1, keepdims=True)
    for r in (1, 2, 3):
        joined = jnp.where(relation == r, z_meta[r], joined)
        spill = jnp.maximum(spill, jnp.max(z_meta[r, 3:4, :], axis=1, keepdims=True))
    metas[0] = joined
    for t in range(3):
        side_meta_copy(t).start()

    def prepare(b):
        keys = jnp.broadcast_to(metas[b, 0:1, :], (128, LAYOUT)).T
        for start, size in STEPS:
            row_key[pl.ds(spot(b, start), size), :] = keys[start : start + size]
        slot = jnp.bitwise_xor(relation[0:1], z) * 32 + metas[b, 2:3, :].astype(jnp.int32)
        places[b] = (
            lax.broadcasted_iota(jnp.int32, (128, LAYOUT), 0) == slot
        ).astype(jnp.float32).astype(jnp.bfloat16)

    def meet(lefts, right, start, size, both=True):
        theirs = blocks[pl.ds(spot(right, start), size), :]
        for first, count in lefts:
            part = pl.ds(first, count)
            scores = lax.dot_general(
                blocks[part, :], theirs, (((1,), (1,)), ((), ())),
                preferred_element_type=jnp.float32,
            )
            my_key = row_key[part, :]
            acc = row_acc[part, :]
            for t in range(size // 128):
                lanes = slice(start + t * 128, start + (t + 1) * 128)
                earlier = metas[right, 0:1, lanes] < my_key
                score = scores[:, t * 128 : (t + 1) * 128]
                acc = jnp.maximum(acc, jnp.where(earlier, score, LOW))
                if both:
                    other = jnp.where(earlier, LOW, score).reshape(count // 8, 8, 128)
                    col_acc[right, :, lanes] = jnp.maximum(
                        col_acc[right, :, lanes], jnp.max(other, axis=0)
                    )
            row_acc[part, :] = acc

    def own_step(s):
        start, size = STEPS[s]
        new = [(spot(0, start), size)]
        for old in STEPS[:s]:
            for right in (0, 2, 3):
                meet(new, right, *old)
        meet(new, 0, start, size, False)

    def side_step(s):
        start, size = STEPS[s]
        s_new, x_new, y_new = [(spot(b, start), size) for b in (1, 2, 3)]
        sides = [s_new, x_new, y_new] if size > 128 else [(s_new[0], 3 * size)]
        for run in STEPS[: s + 1]:
            meet(sides, 0, *run)
            meet([y_new], 2, *run)
        for run in STEPS[:s]:
            meet([x_new], 3, *run)

    def fold(s):
        start, size = STEPS[s]
        for b in range(4):
            turned = row_acc[pl.ds(spot(b, start), size), :].T.reshape(16, 8, size)
            lanes = slice(start, start + size)
            col_acc[b, :, lanes] = jnp.maximum(col_acc[b, :, lanes], jnp.max(turned, axis=0))

    z_copy(1, 0).wait_recv()
    for t in range(3):
        side_copy(t, 1).start()
    prepare(0)
    own_step(0)
    def wait_sides(first, last):
        for k in range(first, last):
            for t in range(3):
                side_copy(t, k).wait_recv()

    done = [max(k for k in range(len(PIECES)) if PIECES[k][0] < a + b) + 1 for a, b in STEPS]
    for k in range(2, len(PIECES)):
        for r in (3, 2):
            z_copy(r, k - 2).wait_recv()
        for t in range(3):
            side_copy(t, k).start()
        if k == 3:
            for t in range(3):
                side_meta_copy(t).wait_recv()
            for b in (1, 2, 3):
                prepare(b)
            wait_sides(0, done[0])
            side_step(0)
            fold(0)
        if k == done[1] - 1:
            own_step(1)
    wait_sides(done[0], done[1])
    side_step(1)
    own_step(2)
    fold(1)
    wait_sides(done[1], len(PIECES))
    side_step(2)
    fold(2)

    for b in range(4):
        value = jnp.max(col_acc[b], axis=0, keepdims=True)
        value = jnp.maximum(value, -1.0)
        parts = []
        for _ in range(3):
            part = value.astype(jnp.bfloat16).astype(jnp.float32)
            parts.append(part)
            value = value - part
        parts.append(jnp.ones_like(value))
        mine = (
            lax.broadcasted_iota(jnp.int32, (8, LAYOUT), 0)
            == metas[b, 1:2, :].astype(jnp.int32)
        ).astype(jnp.float32)
        stacked = jnp.concatenate([mine * part for part in parts], axis=0).astype(jnp.bfloat16)
        found = lax.dot_general(
            stacked, places[b], (((1,), (1,)), ((), ())), preferred_element_type=jnp.float32
        )
        total = (found[16:24] + found[8:16]) + found[0:8]
        fin[:, b, :] = jnp.where(found[24:32] > 0.5, total, -1.0)
    for b in range(4, 8):
        fin[:, b, :] = jnp.broadcast_to(spill, (8, 128))

    for p in range(8):
        me = is_home & (m == p)

        @pl.when(jnp.logical_not(me))
        def _():
            fin_copy(p).start()

        @pl.when(me)
        def _():
            fin_got[here] = fin[p]

    for r in (1, 2, 3):
        z_meta_copy(r).wait_send()
    z_copy(1, 0).wait_send()
    for r in (3, 2):
        for k in range(len(CUTS)):
            z_copy(r, k).wait_send()
    for t in range(3):
        side_meta_copy(t).wait_send()
        for k in range(len(PIECES)):
            side_copy(t, k).wait_send()
    for p in range(8):
        @pl.when(jnp.logical_not(is_home & (m == p)))
        def _():
            fin_copy(p).wait_send()
    for i in range(8):
        @pl.when(jnp.logical_not(is_home & (here == i)))
        def _():
            fin_from(i).wait_recv()

    block = lax.broadcasted_iota(jnp.int32, (1, 128), 1) // 32
    worst = fin_got[0, 4:5, :]
    for i in range(1, 8):
        worst = jnp.maximum(worst, fin_got[i, 4:5, :])
    over[...] = worst[:, :1]
    for xs in range(2):
        for cs in range(2):
            ways = []
            for ys in range(2):
                i = xs * 4 + ys * 2 + cs
                sibling = xs * 4 + ys * 2 + (1 - cs)
                x_holder = (1 - xs) * 4 + ys * 2 + (cs ^ (1 - xs))
                y_holder = xs * 4 + (1 - ys) * 2 + (cs ^ xs ^ (1 - ys))
                ways.append(
                    jnp.maximum(
                        jnp.maximum(fin_got[i, 0:1, :], fin_got[sibling, 1:2, :]),
                        jnp.maximum(fin_got[x_holder, 2:3, :], fin_got[y_holder, 3:4, :]),
                    )
                )
            for half, turns in enumerate(((0, 32, 32, 64), (64, 96, 96, 0))):
                line = ways[0]
                for k in range(4):
                    way = ways[k % 2]
                    turned = pltpu.roll(way, turns[k], 1) if turns[k] else way
                    line = jnp.where(block == k, turned, line)
                row = (xs * 2 + cs) * 2 + half
                out[row : row + 1, :] = line


def routed(embeddings, cluster_id, row_order, assignment, placement):
    rows, width = embeddings.shape
    dma = pltpu.SemaphoreType.DMA
    lines = (rows // 128, 128)
    vmem = pl.BlockSpec(memory_space=pltpu.VMEM)
    return pl.pallas_call(
        routed_kernel,
        out_shape=[jax.ShapeDtypeStruct(shape, jnp.float32) for shape in ((8, 128), (1, 1))],
        in_specs=[
            pl.BlockSpec(memory_space=pltpu.SMEM), pl.BlockSpec(memory_space=pl.ANY),
            vmem, vmem, vmem,
        ],
        out_specs=[vmem, vmem],
        scratch_shapes=[
            pltpu.VMEM((rows, width), jnp.bfloat16),
            pltpu.VMEM((rows, width), jnp.bfloat16),
            pltpu.VMEM((LAYOUT, width), jnp.bfloat16),
            pltpu.VMEM((4 * LAYOUT, width), jnp.bfloat16),
            pltpu.VMEM((8, LAYOUT), jnp.float32),
            pltpu.VMEM((4, 8, LAYOUT), jnp.float32),
            pltpu.VMEM((4, 8, LAYOUT), jnp.float32),
            pltpu.VMEM((4 * LAYOUT, 128), jnp.float32),
            pltpu.VMEM((4 * LAYOUT, 128), jnp.float32),
            pltpu.VMEM((4, 8, LAYOUT), jnp.float32),
            pltpu.VMEM((4, 128, LAYOUT), jnp.bfloat16),
            pltpu.VMEM((8, 8, 128), jnp.float32),
            pltpu.VMEM((8, 8, 128), jnp.float32),
            dma(()),
            dma((4, len(CUTS))), dma((4, len(CUTS))),
            dma((4,)), dma((4,)),
            dma((3, len(PIECES))), dma((3, len(PIECES))),
            dma((3,)), dma((3,)),
            dma((8,)), dma((8,)),
        ],
        compiler_params=pltpu.CompilerParams(
            collective_id=0, has_side_effects=True, vmem_limit_bytes=48 * 1024 * 1024
        ),
    )(
        assignment, embeddings, cluster_id.reshape(lines), row_order.reshape(lines),
        placement.reshape(lines),
    )


def dense(embeddings, cluster_id, row_order, assignment, placement):
    members = lax.axis_size("mem")
    groups = lax.axis_size("grp")
    owners = groups * members
    row_count, feature_count = embeddings.shape
    capacity = max(2, 2 * row_count // owners)
    widened = embeddings.astype(jnp.float32)
    unit_rows = (
        widened
        * lax.rsqrt(jnp.mean(widened * widened, axis=1, keepdims=True) + 1e-06)
        * (1.0 / math.sqrt(feature_count))
    ).astype(jnp.bfloat16)
    meta = jnp.stack([row_order, cluster_id]).astype(jnp.float32)
    best = similarities(unit_rows, meta, groups, members)

    table_hits = cluster_id[:, None] == jnp.arange(assignment.shape[0], dtype=jnp.int32)[None, :]
    group_of = jnp.sum(jnp.where(table_hits, assignment[None, :], 0), axis=1)
    owner_id = group_of * members + placement
    before = jnp.arange(row_count)[None, :] < jnp.arange(row_count)[:, None]
    rank = jnp.sum((before & (owner_id[None, :] == owner_id[:, None])).astype(jnp.int32), axis=1)
    target = owner_id * capacity + rank
    slots = jnp.arange(owners * capacity, dtype=jnp.int32)
    filled = jnp.max(
        jnp.where(slots[:, None] == target[None, :], best, -1.0), axis=1
    )
    return lax.all_to_all(filled, ("grp", "mem"), split_axis=0, concat_axis=0, tiled=True)


def local(*args):
    embeddings, _, _, assignment, _ = args
    shape = (lax.axis_size("grp"), lax.axis_size("mem"), assignment.shape[0]) + embeddings.shape
    if shape != (4, 8, 4, 512, 768):
        return dense(*args)
    found, over = routed(*args)
    return lax.cond(
        over[0, 0] > 0.5, lambda: dense(*args), lambda: found.reshape(found.size)
    )


def solution(mesh):
    return jax.shard_map(
        local,
        mesh=mesh,
        in_specs=(
            P(("grp", "mem"), None),
            P(("grp", "mem")),
            P(("grp", "mem")),
            P(),
            P(("grp", "mem")),
        ),
        out_specs=P(("grp", "mem")),
        check_vma=False,
    )
```

```python
import functools
import math

import jax
import jax.numpy as jnp
from jax import lax
from jax.experimental import pallas as pl
from jax.experimental.pallas import tpu as pltpu
from jax.sharding import PartitionSpec as P

MESH = pl.DeviceIdType.MESH
NZ = 4
CHUNKS = 4
TILE = 256
LOW = -2.0


def flip(index, mask):
    out, bit = index, 1
    while bit <= mask:
        if mask & bit:
            out = out + bit - 2 * bit * (lax.div(index, bit) % 2)
        bit *= 2
    return out


def kernel(
    groups, ys, units, meta, best, planes, zs, plane_meta, z_meta, col_acc, row_acc,
    row_key, row_cluster, back, z_back, z_send, ready_sem, p_send, p_recv, z_ssem, z_rsem,
    pm_send, pm_recv, zm_send, zm_recv, b_send, b_recv, zb_send, zb_recv, relay_sem,
):
    g, m = lax.axis_index("grp"), lax.axis_index("mem")
    z, y = lax.div(m, ys), m % ys
    tiles = (groups // 2) * ys
    count = 2 * tiles
    rows = planes.shape[1]
    part = rows // CHUNKS

    def plane_peer(d):
        j, c = d // 2, d % 2
        return (flip(g, (j // ys) * 2 + c), z * ys + flip(y, j % ys))

    def column_peer(dz):
        return (g, ((z + dz) % NZ) * ys + y)

    load = pltpu.make_async_copy(units, planes.at[0], ready_sem)
    load.start()

    barrier = pltpu.get_barrier_semaphore()
    peers = [plane_peer(d) for d in range(1, count)] + [column_peer(k) for k in range(1, NZ)]
    for peer in peers:
        pl.semaphore_signal(barrier, inc=1, device_id=peer, device_id_type=MESH)
    col_acc[...] = jnp.full(col_acc.shape, LOW, jnp.float32)
    row_acc[...] = jnp.full(row_acc.shape, LOW, jnp.float32)
    plane_meta[0] = meta[...]
    load.wait()
    pl.semaphore_wait(barrier, len(peers))

    def remote(src, dst, ssem, rsem, peer):
        return pltpu.make_async_remote_copy(
            src_ref=src, dst_ref=dst, send_sem=ssem, recv_sem=rsem,
            device_id=peer, device_id_type=MESH,
        )

    def piece(k):
        return pl.ds(k * part, part)

    def own_to_z(k, slot, dz):
        return remote(
            planes.at[0, piece(k)], zs.at[slot, piece(k)], z_ssem.at[slot, k],
            z_rsem.at[slot, k], column_peer(dz),
        )

    def relay(k, src, dst, dz):
        return remote(
            zs.at[src, piece(k)], zs.at[dst, piece(k)], relay_sem.at[src, k],
            z_rsem.at[dst, k], column_peer(dz),
        )

    def to_plane(d):
        return remote(planes.at[0], planes.at[d], p_send.at[d], p_recv.at[d], plane_peer(d))

    def forward(j):
        return remote(
            planes.at[2 * j], planes.at[2 * j + 1], p_send.at[2 * j + 1], p_recv.at[2 * j + 1],
            plane_peer(1),
        )

    meta_copies = [
        remote(meta, plane_meta.at[d], pm_send.at[d], pm_recv.at[d], plane_peer(d))
        for d in range(1, count)
    ] + [
        remote(meta, z_meta.at[s], zm_send.at[s], zm_recv.at[s], column_peer(-1 - s))
        for s in range(2)
    ]
    for copy in meta_copies:
        copy.start()

    to_plane(1).start()

    @pl.when(z >= 1)
    def _():
        for k in range(CHUNKS):
            own_to_z(k, 0, -1).start()

    @pl.when(z <= 1)
    def _():
        for k in range(CHUNKS):
            own_to_z(k, 1, 2).start()

    for j in range(1, tiles):
        to_plane(2 * j).start()

    def spread(a, source):
        row_key[a] = jnp.broadcast_to(source[0:1, :], (128, rows)).T
        row_cluster[a] = jnp.broadcast_to(source[1:2, :], (128, rows)).T

    def pairs(a, left, d, both):
        right = planes[d]
        keys, clusters = plane_meta[d, 0:1, :], plane_meta[d, 1:2, :]

        def step(i, carry):
            here = pl.ds(pl.multiple_of(i * TILE, TILE), TILE)
            scores = lax.dot_general(
                left[here, :], right, (((1,), (1,)), ((), ())),
                preferred_element_type=jnp.float32,
            )
            my_key, my_cluster = row_key[a, here, :], row_cluster[a, here, :]
            acc = row_acc[a, here, :]
            for t in range(rows // 128):
                lanes = slice(t * 128, (t + 1) * 128)
                kept = jnp.where(my_cluster == clusters[:, lanes], scores[:, lanes], LOW)
                earlier = keys[:, lanes] < my_key
                acc = jnp.maximum(acc, jnp.where(earlier, kept, LOW))
                if both:
                    other = jnp.where(earlier, LOW, kept).reshape(TILE // 8, 8, 128)
                    col_acc[d, :, lanes] = jnp.maximum(col_acc[d, :, lanes], jnp.max(other, axis=0))
            row_acc[a, here, :] = acc
            return carry

        lax.fori_loop(0, rows // TILE, step, 0)

    spread(0, meta)
    own = planes.at[0]
    pairs(0, own, 0, False)
    for copy in meta_copies:
        copy.wait()
    to_plane(1).wait_recv()
    pairs(0, own, 1, False)

    for k in range(CHUNKS):
        @pl.when((z == 1) | (z == 2))
        def _():
            own_to_z(k, 0, -1).wait_recv()
            relay(k, 0, 1, -1).start()

        @pl.when(z == 2)
        def _():
            own_to_z(k, 1, 2).wait_recv()
            relay(k, 1, 0, 1).start()

    def plane_step(j, carry):
        pltpu.make_async_copy(planes.at[2 * j], planes.at[2 * j], p_recv.at[2 * j]).wait()
        forward(j).start()
        pairs(0, own, 2 * j, False)
        forward(j).wait_recv()
        pairs(0, own, 2 * j + 1, False)
        return carry

    lax.fori_loop(1, tiles, plane_step, 0)

    for k in range(CHUNKS):
        @pl.when((z == 0) | (z == 3))
        def _():
            own_to_z(k, 0, -1).wait_recv()

        @pl.when(z != 2)
        def _():
            own_to_z(k, 1, 2).wait_recv()

    spread(1, z_meta.at[0])
    spread(2, z_meta.at[1])

    def z1_step(d, carry):
        pairs(1, zs.at[0], d, True)
        return carry

    lax.fori_loop(0, count, z1_step, 0)
    first = lax.div(z, 2) * (count // 2)

    def z2_step(d, carry):
        pairs(2, zs.at[1], d + first, True)
        return carry

    lax.fori_loop(0, count // 2, z2_step, 0)

    def fold(a):
        return jnp.max(row_acc[a].T.reshape(16, 8, rows), axis=0)

    z_send[0] = fold(1)
    z_send[1] = fold(2)
    result_copies = [
        remote(col_acc.at[d], back.at[d], b_send.at[d], b_recv.at[d], plane_peer(d))
        for d in range(1, count)
    ]
    for copy in result_copies:
        copy.start()
    mine = jnp.maximum(fold(0), col_acc[0])
    z_copies = [
        remote(z_send.at[s], z_back.at[s], zb_send.at[s], zb_recv.at[s], column_peer(1 + s))
        for s in range(2)
    ]
    for copy in z_copies:
        copy.start()

    @pl.when(z >= 1)
    def _():
        for k in range(CHUNKS):
            own_to_z(k, 0, -1).wait_send()

    @pl.when(z <= 1)
    def _():
        for k in range(CHUNKS):
            own_to_z(k, 1, 2).wait_send()

    @pl.when((z == 1) | (z == 2))
    def _():
        for k in range(CHUNKS):
            relay(k, 0, 1, -1).wait_send()

    @pl.when(z == 2)
    def _():
        for k in range(CHUNKS):
            relay(k, 1, 0, 1).wait_send()

    to_plane(1).wait_send()
    for j in range(1, tiles):
        to_plane(2 * j).wait_send()
        forward(j).wait_send()

    for copy in result_copies + z_copies:
        copy.wait()
    for d in range(1, count):
        mine = jnp.maximum(mine, back[d])
    mine = jnp.maximum(mine, jnp.maximum(z_back[0], z_back[1]))
    best[...] = jnp.maximum(jnp.max(mine, axis=0, keepdims=True), -1.0)


def similarities(units, meta, groups, members):
    rows, width = units.shape
    ys = members // NZ
    count = groups * ys
    dma = pltpu.SemaphoreType.DMA
    return pl.pallas_call(
        functools.partial(kernel, groups, ys),
        out_shape=jax.ShapeDtypeStruct((1, rows), jnp.float32),
        in_specs=[
            pl.BlockSpec(memory_space=pl.ANY),
            pl.BlockSpec(memory_space=pltpu.VMEM),
        ],
        out_specs=pl.BlockSpec(memory_space=pltpu.VMEM),
        scratch_shapes=[
            pltpu.VMEM((count, rows, width), jnp.bfloat16),
            pltpu.VMEM((2, rows, width), jnp.bfloat16),
            pltpu.VMEM((count, 2, rows), jnp.float32),
            pltpu.VMEM((2, 2, rows), jnp.float32),
            pltpu.VMEM((count, 8, rows), jnp.float32),
            pltpu.VMEM((3, rows, 128), jnp.float32),
            pltpu.VMEM((3, rows, 128), jnp.float32),
            pltpu.VMEM((3, rows, 128), jnp.float32),
            pltpu.VMEM((count, 8, rows), jnp.float32),
            pltpu.VMEM((2, 8, rows), jnp.float32),
            pltpu.VMEM((2, 8, rows), jnp.float32),
            dma(()),
            dma((count,)), dma((count,)),
            dma((2, CHUNKS)), dma((2, CHUNKS)),
            dma((count,)), dma((count,)),
            dma((2,)), dma((2,)),
            dma((count,)), dma((count,)),
            dma((2,)), dma((2,)),
            dma((2, CHUNKS)),
        ],
        compiler_params=pltpu.CompilerParams(
            collective_id=1, has_side_effects=True, vmem_limit_bytes=56 * 1024 * 1024
        ),
    )(units, meta)


HELD = 176
LAYOUT = 768
BIG = 1e9
CUTS = (32, 32, 32, 32, 32, 16)
STEPS = ((0, 384), (384, 256), (640, 128))
NEAR = (176, 176)
BEFORE = [sum(CUTS[:k]) for k in range(len(CUTS))]
FAR = {
    j: [(384 + 2 * skip + (j - 2) * cut, cut) for skip, cut in zip(BEFORE, CUTS)] for j in (2, 3)
}
PIECES = [(0, 176), NEAR] + [(384 + 2 * skip, 2 * cut) for skip, cut in zip(BEFORE, CUTS)]


def relation_of(place):
    relation = jnp.where(place < 176, 0, jnp.where(place < 352, 1, 2))
    for start, cut in FAR[3]:
        relation = jnp.where((place >= start) & (place < start + cut), 3, relation)
    return relation


def spot(b, row):
    start, size = [step for step in STEPS if step[0] <= row][-1]
    return 4 * start + b * size + row - start


def either(a, b):
    return a + b - 2 * a * b


def routed_kernel(
    assignment, embeddings, cluster, order, member, out, over,
    raw, units, sent, blocks, sent_meta, z_meta, metas, row_key, row_acc, col_acc,
    places, fin, fin_got, load_sem, zs, zr, mzs, mzr, ps, pr, mps, mpr, fs, fr,
):
    g, m = lax.axis_index("grp"), lax.axis_index("mem")
    x, c, z, y = lax.div(g, 2), g % 2, lax.div(m, 2), m % 2
    rows, width = raw.shape
    owners, capacity = 32, 32

    load = pltpu.make_async_copy(embeddings, raw, load_sem)
    load.start()

    def device(x, c, z, y):
        return (x * 2 + c, z * 2 + y)

    def column(j):
        return device(x, c, flip(z, j), y)

    side_to = (
        device(x, 1 - c, z, y),
        device(1 - x, either(c, 1 - x), z, y),
        device(x, either(either(c, x), 1 - y), z, 1 - y),
    )
    side_from = (
        device(x, 1 - c, z, y),
        device(1 - x, either(c, x), z, y),
        device(x, either(either(c, x), y), z, 1 - y),
    )
    here = x * 4 + y * 2 + c

    def home(i):
        return device(i // 4, i % 2, g, (i // 2) % 2)

    is_home = z == g
    barrier = pltpu.get_barrier_semaphore()
    for peer in [column(j) for j in (1, 2, 3)] + list(side_from):
        pl.semaphore_signal(barrier, inc=1, device_id=peer, device_id_type=MESH)

    def remote(src, dst, ssem, rsem, peer):
        return pltpu.make_async_remote_copy(
            src_ref=src, dst_ref=dst, send_sem=ssem, recv_sem=rsem,
            device_id=peer, device_id_type=MESH,
        )

    def z_copy(j, k):
        start, size = NEAR if j == 1 else FAR[j][k]
        here = pl.ds(start, size)
        there = pl.ds(spot(0, start), size)
        return remote(sent.at[here], blocks.at[there], zs.at[j, k], zr.at[j, k], column(j))

    def z_meta_copy(j):
        return remote(sent_meta, z_meta.at[j], mzs.at[j], mzr.at[j], column(j))

    def side_copy(t, k):
        start, size = PIECES[k]
        mine, theirs = pl.ds(spot(0, start), size), pl.ds(spot(t + 1, start), size)
        return remote(
            blocks.at[mine], blocks.at[theirs], ps.at[t, k], pr.at[t, k], side_to[t]
        )

    def side_meta_copy(t):
        return remote(metas.at[0], metas.at[t + 1], mps.at[t], mpr.at[t], side_to[t])

    def fin_copy(p):
        return remote(fin.at[p], fin_got.at[here], fs.at[p], fr.at[here], (z, p))

    def fin_from(i):
        return remote(fin.at[0], fin_got.at[i], fs.at[0], fr.at[i], home(i))

    def wide(ref):
        return jnp.concatenate([ref[i : i + 1, :] for i in range(rows // 128)], axis=1)

    ids, keys, mem_of = wide(cluster), wide(order), wide(member)
    group = jnp.zeros_like(ids)
    for k in range(4):
        group = jnp.where(ids == k, assignment[k], group)
    owner = group * 8 + mem_of
    hits = jnp.concatenate(
        [
            (lax.broadcasted_iota(jnp.int32, (owners, rows), 0) == owner).astype(jnp.float32),
            (lax.broadcasted_iota(jnp.int32, (16, rows), 0) == group).astype(jnp.float32),
        ],
        axis=0,
    )
    before = (
        lax.broadcasted_iota(jnp.int32, (128, 128), 0)
        < lax.broadcasted_iota(jnp.int32, (128, 128), 1)
    ).astype(jnp.float32).astype(jnp.bfloat16)
    earlier_hits = jnp.zeros((owners + 16, 1), jnp.float32)
    counts = []
    for k in range(rows // 128):
        part = hits[:, k * 128 : (k + 1) * 128]
        inside = jnp.dot(part.astype(jnp.bfloat16), before, preferred_element_type=jnp.float32)
        counts.append(part * (inside + earlier_hits))
        earlier_hits = earlier_hits + jnp.sum(part, axis=1, keepdims=True)
    counts = jnp.concatenate(counts, axis=1)
    rank = jnp.sum(counts[:owners], axis=0, keepdims=True)
    pos = jnp.sum(counts[owners:], axis=0, keepdims=True).astype(jnp.int32)
    j = jnp.bitwise_xor(group, z)
    high = jnp.where(j >= 3, 1, 0)
    far = jnp.zeros_like(pos)
    for skip, cut in zip(BEFORE, CUTS):
        far = jnp.where(pos >= skip, 384 + skip + cut * high + pos, far)
    target = jnp.where(j == 0, pos, jnp.where(j == 1, 176 + pos, far))
    target = jnp.where(pos < HELD, target, -1)
    spilled = jnp.max(jnp.where(pos < HELD, 0.0, 1.0), axis=1, keepdims=True)

    def chosen(start, size):
        place = lax.broadcasted_iota(jnp.int32, (size, rows), 0) + start
        return (place == target).astype(jnp.float32).astype(jnp.bfloat16)

    facts = jnp.concatenate(
        [
            lax.shift_right_logical(keys, 8).astype(jnp.float32),
            jnp.bitwise_and(keys, 255).astype(jnp.float32),
            mem_of.astype(jnp.float32),
            rank,
            jnp.ones((1, rows), jnp.float32),
            jnp.zeros((11, rows), jnp.float32),
        ],
        axis=0,
    ).astype(jnp.bfloat16)
    for start, size in STEPS:
        lanes = slice(start, start + size)
        sorted_facts = lax.dot_general(
            facts, chosen(start, size), (((1,), (1,)), ((), ())),
            preferred_element_type=jnp.float32,
        )
        held = sorted_facts[4:5] > 0.5
        sent_meta[0:1, lanes] = jnp.where(
            held, sorted_facts[0:1] * 256.0 + sorted_facts[1:2], BIG
        )
        sent_meta[1:2, lanes] = jnp.where(held, sorted_facts[2:3], -1.0)
        sent_meta[2:3, lanes] = sorted_facts[3:4]
        sent_meta[3:4, lanes] = jnp.broadcast_to(spilled, (1, size))
        sent_meta[4:8, lanes] = jnp.zeros((4, size), jnp.float32)

    load.wait()

    def normalise(i, carry):
        part = pl.ds(pl.multiple_of(i * 128, 128), 128)
        widened = raw[part, :].astype(jnp.float32)
        scale = lax.rsqrt(jnp.mean(widened * widened, axis=1, keepdims=True) + 1e-06)
        units[part, :] = (widened * scale * (1.0 / math.sqrt(width))).astype(jnp.bfloat16)
        return carry

    lax.fori_loop(0, rows // 128, normalise, 0)

    def place(start, size):
        picks = chosen(start, size)
        lanes = slice(start, start + size)
        sorted_facts = lax.dot_general(
            facts, picks, (((1,), (1,)), ((), ())), preferred_element_type=jnp.float32
        )
        held = sorted_facts[4:5] > 0.5
        sent_meta[0:1, lanes] = jnp.where(
            held, sorted_facts[0:1] * 256.0 + sorted_facts[1:2], BIG
        )
        sent_meta[1:2, lanes] = jnp.where(held, sorted_facts[2:3], -1.0)
        sent_meta[2:3, lanes] = sorted_facts[3:4]
        sent_meta[3:4, lanes] = jnp.broadcast_to(spilled, (1, size))
        sent_meta[4:8, lanes] = jnp.zeros((4, size), jnp.float32)
        return jnp.dot(
            picks, units[...], preferred_element_type=jnp.float32
        ).astype(jnp.bfloat16)

    sent[pl.ds(384, 256), :] = place(384, 256)
    near = place(0, 384)
    sent[pl.ds(*NEAR), :] = near[176:352]
    blocks[pl.ds(0, 176), :] = near[:176]
    sent[pl.ds(640, 128), :] = place(640, 128)

    pl.semaphore_wait(barrier, 6)

    for r in (1, 2, 3):
        z_meta_copy(r).start()
    z_copy(1, 0).start()
    for k in range(len(CUTS)):
        z_copy(3, k).start()
        z_copy(2, k).start()
    for t in range(3):
        side_copy(t, 0).start()
    for b in range(4):
        for row in (352, 736):
            blocks[pl.ds(spot(b, row), 32), :] = jnp.zeros((32, width), jnp.bfloat16)
    row_acc[...] = jnp.full(row_acc.shape, LOW, jnp.float32)
    col_acc[...] = jnp.full(col_acc.shape, LOW, jnp.float32)

    for r in (1, 2, 3):
        z_meta_copy(r).wait_recv()
    lane = lax.broadcasted_iota(jnp.int32, (8, LAYOUT), 1)
    relation = relation_of(lane)
    joined = sent_meta[...]
    spill = jnp.max(joined[3:4], axis=1, keepdims=True)
    for r in (1, 2, 3):
        joined = jnp.where(relation == r, z_meta[r], joined)
        spill = jnp.maximum(spill, jnp.max(z_meta[r, 3:4, :], axis=1, keepdims=True))
    metas[0] = joined
    for t in range(3):
        side_meta_copy(t).start()

    def prepare(b):
        keys = jnp.broadcast_to(metas[b, 0:1, :], (128, LAYOUT)).T
        for start, size in STEPS:
            row_key[pl.ds(spot(b, start), size), :] = keys[start : start + size]
        slot = jnp.bitwise_xor(relation[0:1], z) * 32 + metas[b, 2:3, :].astype(jnp.int32)
        places[b] = (
            lax.broadcasted_iota(jnp.int32, (128, LAYOUT), 0) == slot
        ).astype(jnp.float32).astype(jnp.bfloat16)

    def meet(lefts, right, start, size, both=True):
        theirs = blocks[pl.ds(spot(right, start), size), :]
        for first, count in lefts:
            part = pl.ds(first, count)
            scores = lax.dot_general(
                blocks[part, :], theirs, (((1,), (1,)), ((), ())),
                preferred_element_type=jnp.float32,
            )
            my_key = row_key[part, :]
            acc = row_acc[part, :]
            for t in range(size // 128):
                lanes = slice(start + t * 128, start + (t + 1) * 128)
                earlier = metas[right, 0:1, lanes] < my_key
                score = scores[:, t * 128 : (t + 1) * 128]
                acc = jnp.maximum(acc, jnp.where(earlier, score, LOW))
                if both:
                    other = jnp.where(earlier, LOW, score).reshape(count // 8, 8, 128)
                    col_acc[right, :, lanes] = jnp.maximum(
                        col_acc[right, :, lanes], jnp.max(other, axis=0)
                    )
            row_acc[part, :] = acc

    def own_step(s):
        start, size = STEPS[s]
        new = [(spot(0, start), size)]
        for old in STEPS[:s]:
            for right in (0, 2, 3):
                meet(new, right, *old)
        meet(new, 0, start, size, False)

    def side_step(s):
        start, size = STEPS[s]
        s_new, x_new, y_new = [(spot(b, start), size) for b in (1, 2, 3)]
        sides = [s_new, x_new, y_new] if size > 128 else [(s_new[0], 3 * size)]
        for run in STEPS[: s + 1]:
            meet(sides, 0, *run)
            meet([y_new], 2, *run)
        for run in STEPS[:s]:
            meet([x_new], 3, *run)

    def fold(s):
        start, size = STEPS[s]
        for b in range(4):
            turned = row_acc[pl.ds(spot(b, start), size), :].T.reshape(16, 8, size)
            lanes = slice(start, start + size)
            col_acc[b, :, lanes] = jnp.maximum(col_acc[b, :, lanes], jnp.max(turned, axis=0))

    z_copy(1, 0).wait_recv()
    for t in range(3):
        side_copy(t, 1).start()
    prepare(0)
    own_step(0)
    def wait_sides(first, last):
        for k in range(first, last):
            for t in range(3):
                side_copy(t, k).wait_recv()

    done = [max(k for k in range(len(PIECES)) if PIECES[k][0] < a + b) + 1 for a, b in STEPS]
    for k in range(2, len(PIECES)):
        for r in (3, 2):
            z_copy(r, k - 2).wait_recv()
        for t in range(3):
            side_copy(t, k).start()
        if k == 4:
            for t in range(3):
                side_meta_copy(t).wait_recv()
            for b in (1, 2, 3):
                prepare(b)
            wait_sides(0, done[0])
            side_step(0)
            fold(0)
        if k == done[1] - 1:
            own_step(1)
    wait_sides(done[0], done[1])
    side_step(1)
    own_step(2)
    fold(1)
    wait_sides(done[1], len(PIECES))
    side_step(2)
    fold(2)

    for b in range(4):
        value = jnp.max(col_acc[b], axis=0, keepdims=True)
        value = jnp.maximum(value, -1.0)
        parts = []
        for _ in range(3):
            part = value.astype(jnp.bfloat16).astype(jnp.float32)
            parts.append(part)
            value = value - part
        parts.append(jnp.ones_like(value))
        mine = (
            lax.broadcasted_iota(jnp.int32, (8, LAYOUT), 0)
            == metas[b, 1:2, :].astype(jnp.int32)
        ).astype(jnp.float32)
        stacked = jnp.concatenate([mine * part for part in parts], axis=0).astype(jnp.bfloat16)
        found = lax.dot_general(
            stacked, places[b], (((1,), (1,)), ((), ())), preferred_element_type=jnp.float32
        )
        total = (found[16:24] + found[8:16]) + found[0:8]
        fin[:, b, :] = jnp.where(found[24:32] > 0.5, total, -1.0)
    for b in range(4, 8):
        fin[:, b, :] = jnp.broadcast_to(spill, (8, 128))

    for p in range(8):
        me = is_home & (m == p)

        @pl.when(jnp.logical_not(me))
        def _():
            fin_copy(p).start()

        @pl.when(me)
        def _():
            fin_got[here] = fin[p]

    for r in (1, 2, 3):
        z_meta_copy(r).wait_send()
    z_copy(1, 0).wait_send()
    for r in (3, 2):
        for k in range(len(CUTS)):
            z_copy(r, k).wait_send()
    for t in range(3):
        side_meta_copy(t).wait_send()
        for k in range(len(PIECES)):
            side_copy(t, k).wait_send()
    for p in range(8):
        @pl.when(jnp.logical_not(is_home & (m == p)))
        def _():
            fin_copy(p).wait_send()
    for i in range(8):
        @pl.when(jnp.logical_not(is_home & (here == i)))
        def _():
            fin_from(i).wait_recv()

    block = lax.broadcasted_iota(jnp.int32, (1, 128), 1) // 32
    worst = fin_got[0, 4:5, :]
    for i in range(1, 8):
        worst = jnp.maximum(worst, fin_got[i, 4:5, :])
    over[...] = worst[:, :1]
    for xs in range(2):
        for cs in range(2):
            ways = []
            for ys in range(2):
                i = xs * 4 + ys * 2 + cs
                sibling = xs * 4 + ys * 2 + (1 - cs)
                x_holder = (1 - xs) * 4 + ys * 2 + (cs ^ (1 - xs))
                y_holder = xs * 4 + (1 - ys) * 2 + (cs ^ xs ^ (1 - ys))
                ways.append(
                    jnp.maximum(
                        jnp.maximum(fin_got[i, 0:1, :], fin_got[sibling, 1:2, :]),
                        jnp.maximum(fin_got[x_holder, 2:3, :], fin_got[y_holder, 3:4, :]),
                    )
                )
            for half, turns in enumerate(((0, 32, 32, 64), (64, 96, 96, 0))):
                line = ways[0]
                for k in range(4):
                    way = ways[k % 2]
                    turned = pltpu.roll(way, turns[k], 1) if turns[k] else way
                    line = jnp.where(block == k, turned, line)
                row = (xs * 2 + cs) * 2 + half
                out[row : row + 1, :] = line


def routed(embeddings, cluster_id, row_order, assignment, placement):
    rows, width = embeddings.shape
    dma = pltpu.SemaphoreType.DMA
    lines = (rows // 128, 128)
    vmem = pl.BlockSpec(memory_space=pltpu.VMEM)
    return pl.pallas_call(
        routed_kernel,
        out_shape=[jax.ShapeDtypeStruct(shape, jnp.float32) for shape in ((8, 128), (1, 1))],
        in_specs=[
            pl.BlockSpec(memory_space=pltpu.SMEM), pl.BlockSpec(memory_space=pl.ANY),
            vmem, vmem, vmem,
        ],
        out_specs=[vmem, vmem],
        scratch_shapes=[
            pltpu.VMEM((rows, width), jnp.bfloat16),
            pltpu.VMEM((rows, width), jnp.bfloat16),
            pltpu.VMEM((LAYOUT, width), jnp.bfloat16),
            pltpu.VMEM((4 * LAYOUT, width), jnp.bfloat16),
            pltpu.VMEM((8, LAYOUT), jnp.float32),
            pltpu.VMEM((4, 8, LAYOUT), jnp.float32),
            pltpu.VMEM((4, 8, LAYOUT), jnp.float32),
            pltpu.VMEM((4 * LAYOUT, 128), jnp.float32),
            pltpu.VMEM((4 * LAYOUT, 128), jnp.float32),
            pltpu.VMEM((4, 8, LAYOUT), jnp.float32),
            pltpu.VMEM((4, 128, LAYOUT), jnp.bfloat16),
            pltpu.VMEM((8, 8, 128), jnp.float32),
            pltpu.VMEM((8, 8, 128), jnp.float32),
            dma(()),
            dma((4, len(CUTS))), dma((4, len(CUTS))),
            dma((4,)), dma((4,)),
            dma((3, len(PIECES))), dma((3, len(PIECES))),
            dma((3,)), dma((3,)),
            dma((8,)), dma((8,)),
        ],
        compiler_params=pltpu.CompilerParams(
            collective_id=0, has_side_effects=True, vmem_limit_bytes=48 * 1024 * 1024
        ),
    )(
        assignment, embeddings, cluster_id.reshape(lines), row_order.reshape(lines),
        placement.reshape(lines),
    )


def dense(embeddings, cluster_id, row_order, assignment, placement):
    members = lax.axis_size("mem")
    groups = lax.axis_size("grp")
    owners = groups * members
    row_count, feature_count = embeddings.shape
    capacity = max(2, 2 * row_count // owners)
    widened = embeddings.astype(jnp.float32)
    unit_rows = (
        widened
        * lax.rsqrt(jnp.mean(widened * widened, axis=1, keepdims=True) + 1e-06)
        * (1.0 / math.sqrt(feature_count))
    ).astype(jnp.bfloat16)
    meta = jnp.stack([row_order, cluster_id]).astype(jnp.float32)
    best = similarities(unit_rows, meta, groups, members)

    table_hits = cluster_id[:, None] == jnp.arange(assignment.shape[0], dtype=jnp.int32)[None, :]
    group_of = jnp.sum(jnp.where(table_hits, assignment[None, :], 0), axis=1)
    owner_id = group_of * members + placement
    before = jnp.arange(row_count)[None, :] < jnp.arange(row_count)[:, None]
    rank = jnp.sum((before & (owner_id[None, :] == owner_id[:, None])).astype(jnp.int32), axis=1)
    target = owner_id * capacity + rank
    slots = jnp.arange(owners * capacity, dtype=jnp.int32)
    filled = jnp.max(
        jnp.where(slots[:, None] == target[None, :], best, -1.0), axis=1
    )
    return lax.all_to_all(filled, ("grp", "mem"), split_axis=0, concat_axis=0, tiled=True)


def local(*args):
    embeddings, _, _, assignment, _ = args
    shape = (lax.axis_size("grp"), lax.axis_size("mem"), assignment.shape[0]) + embeddings.shape
    if shape != (4, 8, 4, 512, 768):
        return dense(*args)
    found, over = routed(*args)
    return lax.cond(
        over[0, 0] > 0.5, lambda: dense(*args), lambda: found.reshape(found.size)
    )


def solution(mesh):
    return jax.shard_map(
        local,
        mesh=mesh,
        in_specs=(
            P(("grp", "mem"), None),
            P(("grp", "mem")),
            P(("grp", "mem")),
            P(),
            P(("grp", "mem")),
        ),
        out_specs=P(("grp", "mem")),
        check_vma=False,
    )
```
